256 devices in a mesh: seq: 32 (over z, y), head: 2 (over core), dp: 4 (over x).
Axes of the slice: x: 4, y: 4, z: 8, core: 2. Of those that a mesh axis runs over, the one named last changes fastest.
Arguments:
- queries: bfloat16 [90112, 2048], P(('dp', 'seq'), 'head'), parts along dimension 0, may hold values from -96 to 96
- out_grad: bfloat16 [90112, 2048], P(('dp', 'seq'), 'head'), parts along dimension 0, may hold values from -16 to 16
- encodings: bfloat16 [1280, 16, 2048], P(('dp', 'seq'), None, 'head'), parts along dimension 0, may hold values from -6 to 6
- key_weight: bfloat16 [2048, 2048], P(None, 'head'), may hold values from -0.125 to 0.125
- value_weight: bfloat16 [2048, 2048], P(None, 'head'), may hold values from -0.125 to 0.125
- neighbours: int32 [1408, 2], P(('dp', 'seq')), parts along dimension 0, may hold values from 0 to 319, as said below
Outputs:
- query_grad: bfloat16 [90112, 2048], P(('dp', 'seq'), 'head'), parts along dimension 0
- encoding_grad: bfloat16 [1280, 16, 2048], P(('dp', 'seq'), None, 'head'), parts along dimension 0
The draws below stay inside these ranges and needn't reach their ends.
There are 4 independent parts, one for each index of `dp`. The reference program is written for one: setup_inputs(seed, part) draws one part's arguments, and reference() takes and returns one part's arrays. A program takes and returns all parts, laid end to end along the dimension named above; an argument that names none is the same for every part. Nothing has to cross between parts.
Inputs may be any that keep to these rules, and one draw needn't show every extreme that they name: `neighbours`: row r of encodings is held by index r // 10 of seq. In each aligned block of 11 spans, at most 2 of the 22 ids belong to one holder, and some holder has exactly 2. A span's two ids differ.
All inputs are finite; a program needn't handle non-finite values.
Results may differ from the reference program's by a relative error of at most 0.011.
Values may be sent and summed in bfloat16 or wider, within the bound.
No kernel may reach another device: no remote copies, remote signals or barrier semaphores. Data moves between devices by JAX's collectives and lax.ppermute only.
A program may use at most 64 MiB of HBM per device.

```python
import math
import jax
import jax.numpy as jnp
from jax import lax

D = 2048
HEADS = 16
SPAN = 64
NBLEN = 16
TOK_DEV = 704
NB_DEV = 10
TOKENS = 22528
SPANS = 352
NROWS = 320
CAP = 2
N_SEQ = 32


def draw_queries(key, part):
    base = jnp.clip(jax.random.normal(jax.random.fold_in(key, 1), (TOKENS, D), jnp.float32), -6.0, 6.0)
    return base.astype(jnp.bfloat16)


def draw_out_grad(key, part):
    base = jnp.clip(4.0 * jax.random.normal(jax.random.fold_in(key, 2), (TOKENS, D), jnp.float32), -16.0, 16.0)
    return base.astype(jnp.bfloat16)


def draw_neighbours(key, part):
    owners_total = NROWS // NB_DEV
    spans_here = TOK_DEV // SPAN
    ref_count = 2 * spans_here
    slot_total = owners_total * CAP
    key_list = jax.random.split(key, 7)
    popular = jnp.where(jax.random.randint(key_list[0], (owners_total,), 0, 4) == 0, 4, 1).astype(jnp.int32)
    slot_owner = jnp.repeat(jnp.arange(owners_total, dtype=jnp.int32), CAP)
    favored = jax.random.randint(key_list[1], (owners_total, 1), 0, owners_total)
    raw = jax.random.randint(key_list[2], (owners_total, slot_total), 0, 4096) * popular[slot_owner][None, :]
    raw = raw + jnp.where(slot_owner[None, :] == favored, 65536, 0)
    ranked = raw * slot_total + jnp.arange(slot_total, dtype=jnp.int32)[None, :]
    _, taken = lax.top_k(ranked, ref_count)
    chosen = slot_owner[taken]
    shuffle = jax.random.randint(key_list[3], (owners_total, ref_count), 0, 65536) * ref_count + jnp.arange(ref_count, dtype=jnp.int32)[None, :]
    order = jnp.argsort(shuffle, axis=1)
    chosen = jnp.take_along_axis(chosen, order, axis=1).reshape(owners_total, spans_here, 2)
    first_row = jax.random.randint(key_list[4], (owners_total, spans_here), 0, NB_DEV)
    other_row = jax.random.randint(key_list[5], (owners_total, spans_here), 0, NB_DEV)
    offset = jax.random.randint(key_list[6], (owners_total, spans_here), 0, NB_DEV - 1)
    second_row = jnp.where(chosen[..., 0] == chosen[..., 1], (first_row + 1 + offset) % NB_DEV, other_row)
    rows_local = jnp.stack([first_row, second_row], axis=-1)
    return (chosen * NB_DEV + rows_local).reshape(SPANS, 2).astype(jnp.int32)


def steps_of(stream_key, extent, shards, smallest, top_value):
    def one(dim, shards_of):
        draws = jax.random.uniform(jax.random.fold_in(jax.random.fold_in(stream_key, 6), dim), (shards_of,), jnp.float32, smallest / len(shards), top_value / len(shards))
        return jnp.repeat(jnp.exp(draws), extent[dim] // shards_of).reshape((-1,) + (1,) * (len(extent) - dim - 1))

    gain = one(*shards[0])
    for cut in shards[1:]:
        gain = gain * one(*cut)
    return gain


def bell_draw(stream_key, extent, width, reach, pieces=(), kind=jnp.bfloat16):
    array = jax.random.normal(stream_key, extent, jnp.float32) * width
    if len(pieces) > 0:
        array = steps_of(stream_key, extent, pieces, -0.22, 0.18) * array
    return jnp.clip(array, min=-reach, max=reach).astype(kind)


def setup_inputs(seed: int = 0, part: int = 0) -> dict:
    key_of = jax.random.split(jax.random.key(seed), 7)
    part_splits = jax.random.split(jax.random.fold_in(key_of[6], part), 7)
    queries = draw_queries(jax.random.fold_in(jax.random.fold_in(key_of[6], part), 71), part)
    out_grad = draw_out_grad(jax.random.fold_in(jax.random.fold_in(key_of[6], part), 71), part)
    encodings = bell_draw(part_splits[2], (NROWS, NBLEN, D), 1.0, 6.0, ((0, 32), (2, 2)))
    key_weight = bell_draw(key_of[3], (D, D), D ** -0.5, 0.125, ((1, 2),))
    value_weight = bell_draw(key_of[4], (D, D), D ** -0.5, 0.125, ((1, 2),))
    neighbours = draw_neighbours(jax.random.fold_in(jax.random.fold_in(key_of[6], part), 71), part)
    return {"queries": queries, "out_grad": out_grad, "encodings": encodings, "key_weight": key_weight, "value_weight": value_weight, "neighbours": neighbours}


def round_trip(values):
    return lax.optimization_barrier(values.astype(jnp.bfloat16)).astype(jnp.float32)

def reference(queries, out_grad, encodings, key_weight, value_weight, neighbours):
    spans_here = TOK_DEV // SPAN
    ref_count = 2 * spans_here
    head_size = D // HEADS
    scaling = 1.0 / math.sqrt(head_size)
    key_full = key_weight.astype(jnp.float32)
    value_full = value_weight.astype(jnp.float32)

    def per_block(totals, block_index):
        start = block_index * TOK_DEV
        query_rows = lax.dynamic_slice_in_dim(queries, start, TOK_DEV, 0).astype(jnp.float32)
        grad_rows = lax.dynamic_slice_in_dim(out_grad, start, TOK_DEV, 0).astype(jnp.float32)
        chosen = lax.dynamic_slice_in_dim(neighbours, block_index * spans_here, spans_here, 0).reshape(ref_count).astype(jnp.int32)
        picked = jnp.take(encodings, chosen, axis=0).astype(jnp.float32)
        keys = round_trip(jnp.einsum('rld,de->rle', picked, key_full))
        values = round_trip(jnp.einsum('rld,de->rle', picked, value_full))
        query_heads = query_rows.reshape(spans_here, SPAN, HEADS, head_size)
        grad_heads = grad_rows.reshape(spans_here, SPAN, HEADS, head_size)
        key_heads = keys.reshape(spans_here, 2 * NBLEN, HEADS, head_size)
        value_heads = values.reshape(spans_here, 2 * NBLEN, HEADS, head_size)
        scores = jnp.einsum('cthd,cuhd->chtu', query_heads, key_heads) * scaling
        scores = scores - lax.optimization_barrier(jnp.max(scores, axis=-1, keepdims=True))
        raised = jnp.exp(scores)
        probs = raised / lax.optimization_barrier(jnp.sum(raised, axis=-1, keepdims=True))
        probs_b = round_trip(probs)
        attended = jnp.einsum('chtu,cuhd->cthd', probs_b, value_heads)
        delta = jnp.transpose(lax.optimization_barrier(jnp.sum(grad_heads * attended, axis=-1)), (0, 2, 1))
        dprobs = jnp.einsum('cthd,cuhd->chtu', grad_heads, value_heads)
        dscores = round_trip(probs * (dprobs - delta[..., None]))
        query_part = (jnp.einsum('chtu,cuhd->cthd', dscores, key_heads) * scaling).astype(jnp.bfloat16)
        key_grad = round_trip(jnp.einsum('chtu,cthd->cuhd', dscores, query_heads) * scaling)
        value_grad = round_trip(jnp.einsum('chtu,cthd->cuhd', probs_b, grad_heads))
        key_grad = key_grad.reshape(ref_count, NBLEN, D)
        value_grad = value_grad.reshape(ref_count, NBLEN, D)
        ref_grad = round_trip(jnp.einsum('rle,de->rld', key_grad, key_full) + jnp.einsum('rle,de->rld', value_grad, value_full))
        totals = totals.at[chosen].add(ref_grad)
        return (totals, query_part.reshape(TOK_DEV, D))
    initial = jnp.zeros((NROWS, NBLEN, D), jnp.float32)
    totals, query_parts = lax.scan(per_block, initial, jnp.arange(N_SEQ, dtype=jnp.int32))
    return (query_parts.reshape(TOKENS, D), totals.astype(jnp.bfloat16))
```

```python
import math

import jax
import jax.numpy as jnp
from jax import lax
from jax.experimental import pallas as pl
from jax.experimental.pallas import tpu as pltpu
from jax.sharding import PartitionSpec as P

D = 2048
HEADS = 16
NY = 4
CAP = 2


SMEM = pl.BlockSpec(memory_space=pltpu.SMEM)
VMEM = pl.BlockSpec(memory_space=pltpu.VMEM)
BF = jnp.bfloat16
F32 = jnp.float32


def planes_of(step, nz):
    if step == 0 or 2 * step == nz:
        return (step,)
    return (step, nz - step)


def ring(seq, dz, dy):
    nz = seq // NY
    pairs = []
    for z in range(nz):
        for y in range(NY):
            pairs.append((z * NY + y, ((z + dz) % nz) * NY + (y + dy) % NY))
    return pairs


def pick_rows(table, blocks, step, nz, split):
    planes = planes_of(step, nz)
    count = CAP * len(planes)
    tail = blocks[0].shape[1:]

    def body(t_ref, *refs):
        ins, outs = refs[: len(blocks)], refs[len(blocks) :]
        for j in range(NY):
            for p, delta in enumerate(planes):
                for s in range(CAP):
                    row = jnp.maximum(t_ref[j, delta * CAP + s], 0)
                    k = p * CAP + s
                    if split:
                        cut = ins[0].shape[0]

                        @pl.when(row < cut)
                        def _():
                            outs[j][k] = ins[0][jnp.minimum(row, cut - 1)]

                        @pl.when(row >= cut)
                        def _():
                            outs[j][k] = ins[1][jnp.maximum(row - cut, 0)]

                    else:
                        outs[j][k] = ins[p][row]

    return pl.pallas_call(
        body,
        in_specs=[SMEM] + [VMEM] * len(blocks),
        out_specs=[VMEM] * NY,
        out_shape=[jax.ShapeDtypeStruct((count,) + tail, BF)] * NY,
        name=f"pick{step}",
    )(table, *blocks)


def compact(ref_of, groups, nz, ref_count):
    flat = [a for group in groups for a in group]
    tail = flat[0].shape[1:]

    def body(r_ref, *refs):
        ins, out = refs[:-1], refs[-1]
        for step in range(len(groups)):
            for j in range(NY):
                for p, delta in enumerate(planes_of(step, nz)):
                    for s in range(CAP):
                        r = r_ref[j, delta * CAP + s]

                        @pl.when(r >= 0)
                        def _():
                            out[jnp.maximum(r, 0)] = ins[step * NY + j][p * CAP + s]

    return pl.pallas_call(
        body,
        in_specs=[SMEM] + [VMEM] * len(flat),
        out_specs=VMEM,
        out_shape=jax.ShapeDtypeStruct((ref_count,) + tail, BF),
        name="compact",
    )(ref_of, *flat)


def spread(ref_of, own, other, nz, steps):
    tail = own.shape[1:]
    shapes = []
    for step in range(steps):
        count = CAP * len(planes_of(step, nz))
        shapes += [jax.ShapeDtypeStruct((count,) + tail, BF)] * NY

    def body(r_ref, own_ref, other_ref, *outs):
        for step in range(steps):
            for j in range(NY):
                for p, delta in enumerate(planes_of(step, nz)):
                    for s in range(CAP):
                        r = r_ref[j, delta * CAP + s]

                        @pl.when(r >= 0)
                        def _():
                            at = jnp.maximum(r, 0)
                            total = own_ref[at] + other_ref[at].astype(F32)
                            outs[step * NY + j][p * CAP + s] = total.astype(BF)

    flat = pl.pallas_call(
        body,
        in_specs=[SMEM, VMEM, VMEM],
        out_specs=[VMEM] * len(shapes),
        out_shape=shapes,
        name="spread",
    )(ref_of, own, other)
    return [flat[step * NY : (step + 1) * NY] for step in range(steps)]


def gather_grads(table, parts, before, step, nz, rows_here):
    planes = planes_of(step, nz)
    tail = parts[0].shape[1:]
    cut = rows_here // 2
    far = 2 * step == nz
    if far:
        shapes = [(cut,) + tail, (rows_here - cut,) + tail]
    else:
        shapes = [(rows_here,) + tail] * len(planes)

    def body(t_ref, *refs):
        ins = refs[:NY]
        prev = refs[NY : NY + len(before)]
        outs = refs[NY + len(before) : -1]
        acc = refs[-1]
        for p, delta in enumerate(planes):
            acc[p] = jnp.zeros((rows_here,) + tail, F32)
        if step == 0:
            acc[0] = prev[0][...].astype(F32) + prev[1][...].astype(F32)
        elif prev:
            if prev[0].shape[0] == rows_here:
                acc[0] = prev[0][...].astype(F32)
                acc[1] = prev[1][...].astype(F32)
            else:
                acc[0, :cut] = prev[0][...].astype(F32)
                acc[1, cut:] = prev[1][...].astype(F32)
        for j in range(NY):
            for p, delta in enumerate(planes):
                for s in range(CAP):
                    row = t_ref[j, delta * CAP + s]

                    @pl.when(row >= 0)
                    def _():
                        at = jnp.maximum(row, 0)
                        acc[p, at] = acc[p, at] + ins[j][p * CAP + s].astype(F32)

        if far:
            outs[0][...] = acc[0, :cut].astype(BF)
            outs[1][...] = acc[0, cut:].astype(BF)
        else:
            for p in range(len(planes)):
                outs[p][...] = acc[p].astype(BF)

    return pl.pallas_call(
        body,
        in_specs=[SMEM] + [VMEM] * (NY + len(before)),
        out_specs=[VMEM] * len(shapes),
        out_shape=[jax.ShapeDtypeStruct(s, BF) for s in shapes],
        scratch_shapes=[pltpu.VMEM((len(planes), rows_here) + tail, F32)],
        name=f"gather{step}",
    )(table, *parts, *before)


def core_step(head, own, other, key_weight, value_weight, queries, out_grad, spans, head_size):
    rows, half = own.shape
    tok = queries.shape[0] // spans
    per = rows // spans
    heads_here = half // head_size
    scaling = 1.0 / math.sqrt(head_size)
    nt = (((1,), (1,)), ((), ()))
    tn = (((0,), (0,)), ((), ()))

    def body(
        h_ref, own_ref, oth_ref, wk_ref, wv_ref, q_ref, g_ref,
        dq_ref, pown_ref, poth_ref, k_ref, v_ref, dk_ref, dv_ref,
    ):
        i = pl.program_id(0)
        mine = pl.ds(pl.multiple_of(h_ref[0] * half, half), half)
        theirs = pl.ds(pl.multiple_of((1 - h_ref[0]) * half, half), half)

        @pl.when(i == 0)
        def _():
            for w_ref, out in ((wk_ref, k_ref), (wv_ref, v_ref)):
                total = jnp.dot(own_ref[...], w_ref[mine, :], preferred_element_type=F32)
                total += jnp.dot(oth_ref[...], w_ref[theirs, :], preferred_element_type=F32)
                out[...] = total.astype(BF)

        here = pl.ds(pl.multiple_of(i * per, per), per)
        for n in range(heads_here):
            cols = slice(n * head_size, (n + 1) * head_size)
            q = q_ref[:, cols]
            g = g_ref[:, cols]
            k = k_ref[here, cols]
            v = v_ref[here, cols]
            scores = lax.dot_general(k, q, nt, preferred_element_type=F32) * scaling
            scores = scores - jnp.max(scores, axis=0, keepdims=True)
            raised = jnp.exp(scores)
            probs = raised / jnp.sum(raised, axis=0, keepdims=True)
            probs_b = probs.astype(BF)
            dprobs = lax.dot_general(v, g, nt, preferred_element_type=F32)
            delta = jnp.sum(probs_b.astype(F32) * dprobs, axis=0, keepdims=True)
            ds = (probs * (dprobs - delta)).astype(BF)
            dq = lax.dot_general(ds, k, tn, preferred_element_type=F32) * scaling
            dq_ref[:, cols] = dq.astype(BF)
            dk = jnp.dot(ds, q, preferred_element_type=F32) * scaling
            dk_ref[here, cols] = dk.astype(BF)
            dv = jnp.dot(probs_b, g, preferred_element_type=F32)
            dv_ref[here, cols] = dv.astype(BF)

        @pl.when(i == spans - 1)
        def _():
            for at, out in ((theirs, poth_ref), (mine, pown_ref)):
                total = lax.dot_general(dk_ref[...], wk_ref[at, :], nt, preferred_element_type=F32)
                total += lax.dot_general(
                    dv_ref[...], wv_ref[at, :], nt, preferred_element_type=F32
                )
                out[...] = total.astype(out.dtype)

    once = pl.Buffered(1)

    def whole(shape):
        return pl.BlockSpec(shape, lambda i: (0,) * len(shape), pipeline_mode=once)

    span_block = pl.BlockSpec((tok, half), lambda i: (i, 0))
    return pl.pallas_call(
        body,
        grid=(spans,),
        in_specs=[
            SMEM,
            whole((rows, half)),
            whole((rows, half)),
            whole(key_weight.shape),
            whole(value_weight.shape),
            span_block,
            span_block,
        ],
        out_specs=[span_block, whole((rows, half)), whole((rows, half))],
        out_shape=[
            jax.ShapeDtypeStruct(queries.shape, BF),
            jax.ShapeDtypeStruct((rows, half), F32),
            jax.ShapeDtypeStruct((rows, half), BF),
        ],
        scratch_shapes=[pltpu.VMEM((rows, half), BF)] * 4,
        name="core_step",
    )(head.reshape(1), own, other, key_weight, value_weight, queries, out_grad)


def on_device(queries, out_grad, encodings, key_weight, value_weight, neighbours):
    seq = lax.axis_size("seq")
    nz = seq // NY
    far = nz // 2
    index = lax.axis_index("seq")
    head = lax.axis_index("head").astype(jnp.int32)
    z0 = index // NY
    y0 = index % NY
    spans = neighbours.shape[0]
    ref_count = 2 * spans
    rows_here, length, half = encodings.shape
    cut = rows_here // 2

    def move(x, dz, dy):
        return lax.ppermute(x, "seq", ring(seq, dz, dy))

    def swap(x):
        return lax.ppermute(x, "head", [(0, 1), (1, 0)])

    ids = neighbours.reshape(ref_count)
    owner = ids // rows_here
    local = ids % rows_here
    refs = jnp.arange(ref_count, dtype=jnp.int32)
    same = (owner[:, None] == owner[None, :]) & (refs[None, :] < refs[:, None])
    rank = jnp.sum(same.astype(jnp.int32), axis=1)
    code = (((y0 - owner % NY) % NY) * nz + (owner // NY - z0) % nz) * CAP + rank
    slots = jnp.arange(NY * nz * CAP, dtype=jnp.int32)
    match = slots[:, None] == code[None, :]
    wanted = jnp.sum(jnp.where(match, local[None, :] + 1, 0), axis=1) - 1
    ref_of = jnp.sum(jnp.where(match, refs[None, :] + 1, 0), axis=1) - 1
    wanted = wanted.reshape(NY, nz * CAP)
    ref_of = ref_of.reshape(NY, nz * CAP)
    table = [wanted[0:1]] + [move(wanted[j : j + 1], 0, -j) for j in range(1, NY)]
    table = jnp.concatenate(table, axis=0)

    ahead = behind = encodings
    groups = []
    for step in range(far + 1):
        if step == far:
            behind, ahead = move(behind[:cut], 1, 0), move(ahead[cut:], -1, 0)
            blocks = (behind, ahead)
        elif step > 0:
            behind, ahead = move(behind, 1, 0), move(ahead, -1, 0)
            blocks = (ahead, behind)
        else:
            blocks = (encodings,)
        picked = pick_rows(table, blocks, step, nz, step == far)
        groups.append([picked[0]] + [move(picked[j], 0, j) for j in range(1, NY)])

    own = compact(ref_of, groups, nz, ref_count)
    other = swap(own)
    flat = (ref_count * length, half)
    query_grad, partial_own, partial_other = core_step(
        head, own.reshape(flat), other.reshape(flat), key_weight, value_weight,
        queries, out_grad, spans, D // HEADS,
    )
    came = swap(partial_other)
    shape = (ref_count, length, half)
    outgoing = spread(ref_of, partial_own.reshape(shape), came.reshape(shape), nz, far + 1)

    before = ()
    for step in range(far, -1, -1):
        parts = [outgoing[step][0]] + [move(outgoing[step][j], 0, -j) for j in range(1, NY)]
        total = gather_grads(table, parts, before, step, nz, rows_here)
        if step > 0:
            before = (move(total[0], 1, 0), move(total[1], -1, 0))
    return (query_grad, total[0])


def solution(mesh):
    return jax.shard_map(
        on_device,
        mesh=mesh,
        in_specs=(
            P(("dp", "seq"), "head"),
            P(("dp", "seq"), "head"),
            P(("dp", "seq"), None, "head"),
            P(None, "head"),
            P(None, "head"),
            P(("dp", "seq"), None),
        ),
        out_specs=(P(("dp", "seq"), "head"), P(("dp", "seq"), None, "head")),
        check_vma=False,
    )
```

```python
import math

import jax
import jax.numpy as jnp
from jax import lax
from jax.experimental import pallas as pl
from jax.experimental.pallas import tpu as pltpu
from jax.sharding import PartitionSpec as P


D = 2048
HEADS = 16
NY = 4
CAP = 2


SMEM = pl.BlockSpec(memory_space=pltpu.SMEM)
VMEM = pl.BlockSpec(memory_space=pltpu.VMEM)
ANY = pl.BlockSpec(memory_space=pl.ANY)
BF = jnp.bfloat16
SMALL = pltpu.CompilerParams(vmem_limit_bytes=8 << 20)
F32 = jnp.float32

OUT = ((0, 1, 2), (3, 4))


def planes_of(step, nz):
    if step == 0 or 2 * step == nz:
        return (step,)
    return (step, nz - step)


def slots_of(phase, nz):
    return [(d, s) for step in phase for d in planes_of(step, nz) for s in range(CAP)]


def ring(seq, dz, dy):
    nz = seq // NY
    pairs = []
    for z in range(nz):
        for y in range(NY):
            pairs.append((z * NY + y, ((z + dz) % nz) * NY + (y + dy) % NY))
    return pairs


def pick_rows(table, place, blocks, phase, nz):
    slots = slots_of(phase, nz)
    flat, where = [], {}
    for d, pieces in blocks.items():
        where[d] = []
        start = 0
        for a in pieces:
            where[d].append((len(flat), start, a.shape[0]))
            start += a.shape[0]
            flat.append(a)
    tail = flat[0].shape[1:]

    def body(t_ref, p_ref, *refs):
        ins, outs = refs[: len(flat)], refs[len(flat) :]
        for j in range(NY):
            for k, (d, s) in enumerate(slots):
                row = jnp.maximum(t_ref[j, (p_ref[0] + d) % nz * CAP + s], 0)
                if len(where[d]) == 1:
                    outs[j][k] = ins[where[d][0][0]][row]
                    continue
                for n, start, size in where[d]:

                    @pl.when((row >= start) & (row < start + size))
                    def _():
                        outs[j][k] = ins[n][jnp.clip(row - start, 0, size - 1)]

    return pl.pallas_call(
        body,
        in_specs=[SMEM, SMEM] + [VMEM] * len(flat),
        out_specs=[VMEM] * NY,
        out_shape=[jax.ShapeDtypeStruct((len(slots),) + tail, BF)] * NY,
        name="pick",
        compiler_params=SMALL,
    )(table, place, *flat)


def compact(ref_of, place, groups, nz, ref_count):
    flat = [a for group in groups for a in group]
    tail = flat[0].shape[1:]

    def body(r_ref, p_ref, *refs):
        ins, out = refs[:-1], refs[-1]
        for n, phase in enumerate(OUT):
            for j in range(NY):
                for k, (d, s) in enumerate(slots_of(phase, nz)):
                    r = r_ref[j, (p_ref[0] + d) % nz * CAP + s]

                    @pl.when(r >= 0)
                    def _():
                        out[jnp.maximum(r, 0)] = ins[n * NY + j][k]

    return pl.pallas_call(
        body,
        in_specs=[SMEM, SMEM] + [VMEM] * len(flat),
        out_specs=VMEM,
        out_shape=jax.ShapeDtypeStruct((ref_count,) + tail, BF),
        name="compact",
        compiler_params=SMALL,
    )(ref_of, place, *flat)


def spread(ref_of, place, own, other, seq):
    tail = own.shape[1:]
    nz = seq // NY

    def body(r_ref, p_ref, own_ref, other_ref, out):
        for j in range(NY):
            for d in range(nz):
                holder = d * NY + (p_ref[1] + NY - j) % NY
                for s in range(CAP):
                    r = r_ref[j, d * CAP + s]

                    @pl.when(r >= 0)
                    def _():
                        at = jnp.maximum(r, 0)
                        total = own_ref[at] + other_ref[at].astype(F32)
                        out[holder * CAP + s] = total.astype(BF)

    return pl.pallas_call(
        body,
        in_specs=[SMEM, SMEM, VMEM, VMEM],
        out_specs=VMEM,
        out_shape=jax.ShapeDtypeStruct((seq * CAP,) + tail, BF),
        name="spread",
        compiler_params=SMALL,
    )(ref_of, place, own, other)


def combine(named, place, came, rows_here):
    slots = came.shape[0]
    tail = came.shape[1:]

    def body(n_ref, p_ref, in_ref, out, acc):
        def clear(r, carry):
            acc[r] = jnp.zeros(tail, F32)
            return carry

        def add(k, carry):
            reader = k // CAP
            j = (reader % NY + NY - p_ref[1]) % NY
            row = n_ref[j, reader // NY * CAP + k % CAP]

            @pl.when(row >= 0)
            def _():
                at = jnp.maximum(row, 0)
                acc[at] = acc[at] + in_ref[k].astype(F32)

            return carry

        def drain(r, carry):
            out[r] = acc[r].astype(BF)
            return carry

        lax.fori_loop(0, rows_here, clear, 0)
        lax.fori_loop(0, slots, add, 0)
        lax.fori_loop(0, rows_here, drain, 0)

    return pl.pallas_call(
        body,
        in_specs=[SMEM, SMEM, VMEM],
        out_specs=VMEM,
        out_shape=jax.ShapeDtypeStruct((rows_here,) + tail, BF),
        scratch_shapes=[pltpu.VMEM((rows_here,) + tail, F32)],
        name="combine",
        compiler_params=SMALL,
    )(named, place, came)


def fetch(*arrays):
    count = len(arrays)

    def body(*refs):
        sem = refs[-1]
        copies = [
            pltpu.make_async_copy(refs[n], refs[count + n], sem.at[n]) for n in range(count)
        ]
        for copy in copies:
            copy.start()
        for copy in copies:
            copy.wait()

    return pl.pallas_call(
        body,
        in_specs=[pl.BlockSpec(memory_space=pltpu.HBM)] * count,
        out_specs=[VMEM] * count,
        out_shape=[pltpu.VMEM(a.shape, a.dtype) for a in arrays],
        scratch_shapes=[pltpu.SemaphoreType.DMA((count,))],
        compiler_params=SMALL,
        name="fetch",
    )(*arrays)


def core_step(place, own, other, key_weight, value_weight, queries, out_grad, spans, head_size):
    rows, half = own.shape
    tok = queries.shape[0] // spans
    per = rows // spans
    heads = half // head_size
    scaling = 1.0 / math.sqrt(head_size)
    nt = (((1,), (1,)), ((), ()))
    tn = (((0,), (0,)), ((), ()))
    cols = [slice(n * head_size, (n + 1) * head_size) for n in range(heads)]

    def body(
        p_ref, own_ref, oth_ref, wk_ref, wv_ref, q_ref, g_ref, dq_hbm, pown_ref, poth_ref,
        dq_ref, k_ref, v_ref, dk_ref, dv_ref, sem,
    ):
        mine = pl.ds(pl.multiple_of(p_ref[2] * half, half), half)
        theirs = pl.ds(pl.multiple_of((1 - p_ref[2]) * half, half), half)
        for w_ref, out in ((wk_ref, k_ref), (wv_ref, v_ref)):
            total = jnp.dot(own_ref[...], w_ref[mine, :], preferred_element_type=F32)
            total += jnp.dot(oth_ref[...], w_ref[theirs, :], preferred_element_type=F32)
            out[...] = total.astype(BF)

        def span(u, carry):
            here = pl.ds(pl.multiple_of(u * per, per), per)
            there = pl.ds(pl.multiple_of(u * tok, tok), tok)
            q = [q_ref[there, c] for c in cols]
            g = [g_ref[there, c] for c in cols]
            k = [k_ref[here, c] for c in cols]
            v = [v_ref[here, c] for c in cols]
            scores = [
                lax.dot_general(a, b, nt, preferred_element_type=F32) for a, b in zip(k, q)
            ]
            dprobs = [
                lax.dot_general(a, b, nt, preferred_element_type=F32) for a, b in zip(v, g)
            ]
            probs_b, ds = [], []
            for sc, dp in zip(scores, dprobs):
                sc = sc * scaling
                raised = jnp.exp(sc - jnp.max(sc, axis=0, keepdims=True))
                probs = raised / jnp.sum(raised, axis=0, keepdims=True)
                pb = probs.astype(BF)
                delta = jnp.sum(pb.astype(F32) * dp, axis=0, keepdims=True)
                probs_b.append(pb)
                ds.append((probs * (dp - delta)).astype(BF))
            for n, c in enumerate(cols):
                dk = jnp.dot(ds[n], q[n], preferred_element_type=F32) * scaling
                dv = jnp.dot(probs_b[n], g[n], preferred_element_type=F32)
                dq = lax.dot_general(ds[n], k[n], tn, preferred_element_type=F32) * scaling
                dk_ref[here, c] = dk.astype(BF)
                dv_ref[here, c] = dv.astype(BF)
                dq_ref[there, c] = dq.astype(BF)
            return carry

        lax.fori_loop(0, spans, span, 0)
        store = pltpu.make_async_copy(dq_ref, dq_hbm, sem.at[0])
        store.start()
        for at, out in ((theirs, poth_ref), (mine, pown_ref)):
            total = lax.dot_general(dk_ref[...], wk_ref[at, :], nt, preferred_element_type=F32)
            total += lax.dot_general(dv_ref[...], wv_ref[at, :], nt, preferred_element_type=F32)
            out[...] = total.astype(out.dtype)
        store.wait()

    return pl.pallas_call(
        body,
        in_specs=[SMEM, VMEM, VMEM, VMEM, VMEM, VMEM, VMEM],
        out_specs=[ANY, VMEM, VMEM],
        compiler_params=pltpu.CompilerParams(vmem_limit_bytes=16 << 20),
        out_shape=[
            jax.ShapeDtypeStruct(queries.shape, BF),
            jax.ShapeDtypeStruct((rows, half), F32),
            jax.ShapeDtypeStruct((rows, half), BF),
        ],
        scratch_shapes=[pltpu.VMEM(queries.shape, BF)]
        + [pltpu.VMEM((rows, half), BF)] * 4
        + [pltpu.SemaphoreType.DMA((1,))],
        name="core_step",
    )(place, own, other, key_weight, value_weight, queries, out_grad)


def slot_tables(ids, y0, nz, rows_here):
    count = ids.shape[1]
    owner = ids // rows_here
    local = ids % rows_here
    plane = owner // NY
    column = owner % NY
    refs = jnp.arange(count, dtype=jnp.int32)
    same = (owner[:, :, None] == owner[:, None, :]) & (refs[None, None, :] < refs[None, :, None])
    rank = jnp.sum(same.astype(jnp.int32), axis=2)
    code = plane * CAP + rank
    slots = jnp.arange(nz * CAP, dtype=jnp.int32)
    hit = (slots[None, :, None] == code[:, None, :]) & (column == y0)[:, None, :]
    table = jnp.sum(jnp.where(hit, local[:, None, :] + 1, 0), axis=2) - 1
    back = (y0 - column[0]) % NY
    sides = jnp.arange(NY, dtype=jnp.int32)
    mine = (slots[None, :, None] == code[0][None, None, :]) & (
        sides[:, None, None] == back[None, None, :]
    )
    ref_of = jnp.sum(jnp.where(mine, refs[None, None, :] + 1, 0), axis=2) - 1
    return table, ref_of


def whole_step(queries, out_grad, encodings, key_weight, value_weight, neighbours):
    seq = lax.axis_size("seq")
    nz = seq // NY
    far = nz // 2
    index = lax.axis_index("seq")
    head = lax.axis_index("head").astype(jnp.int32)
    z0 = index // NY
    y0 = index % NY
    spans = neighbours.shape[0]
    ref_count = 2 * spans
    rows_here, length, half = encodings.shape
    cut = rows_here // 2

    def move(x, dz, dy):
        return lax.ppermute(x, "seq", ring(seq, dz, dy))

    def swap(x):
        return lax.ppermute(x, "head", [(0, 1), (1, 0)])

    place = jnp.stack([z0, y0, head]).astype(jnp.int32)

    blocks = {0: [encodings]}
    ahead = behind = encodings
    readers = None
    for step in range(1, far + 1):
        if step == far:
            ahead, behind = ahead[cut:], behind[:cut]
        behind = move(behind, 1, 0)
        ahead = move(ahead, -1, 0)
        if step == far:
            blocks[far] = [behind, ahead]
        else:
            blocks[step], blocks[nz - step] = [ahead], [behind]
        if readers is None:
            ids = neighbours.reshape(1, ref_count)
            readers = [ids] + [move(ids, 0, -j) for j in range(1, NY)]
            table, ref_of = slot_tables(jnp.concatenate(readers, axis=0), y0, nz, rows_here)
    groups = []
    for phase in OUT:
        need = {d: blocks[d] for step in phase for d in planes_of(step, nz)}
        picked = pick_rows(table, place, need, phase, nz)
        groups.append([picked[0]] + [move(picked[j], 0, j) for j in range(1, NY)])

    own = compact(ref_of, place, groups, nz, ref_count)
    other = swap(own)
    lines = [[z * NY + y for z in range(nz)] for y in range(NY)]
    named = lax.all_to_all(
        table.reshape(NY, nz, CAP), "seq", 1, 1, axis_index_groups=lines, tiled=True
    ).reshape(NY, nz * CAP)

    flat = (ref_count * length, half)
    key_weight, value_weight, queries, out_grad = (
        pltpu.with_memory_space_constraint(a, pltpu.VMEM)
        for a in fetch(
            *(
                pltpu.with_memory_space_constraint(a, pltpu.HBM)
                for a in (key_weight, value_weight, queries, out_grad)
            )
        )
    )
    query_grad, partial_own, partial_other = core_step(
        place, own.reshape(flat), other.reshape(flat), key_weight, value_weight,
        queries, out_grad, spans, D // HEADS,
    )
    came = swap(partial_other)
    shape = (ref_count, length, half)
    outgoing = spread(ref_of, place, partial_own.reshape(shape), came.reshape(shape), seq)
    outgoing = outgoing.reshape(seq, CAP, length, half)
    back = lax.all_to_all(outgoing, "seq", split_axis=0, concat_axis=0, tiled=True)
    total = combine(named, place, back.reshape(seq * CAP, length, half), rows_here)
    return (query_grad, total)


def solution(mesh):
    return jax.shard_map(
        whole_step,
        mesh=mesh,
        in_specs=(
            P(("dp", "seq"), "head"),
            P(("dp", "seq"), "head"),
            P(("dp", "seq"), None, "head"),
            P(None, "head"),
            P(None, "head"),
            P(("dp", "seq"), None),
        ),
        out_specs=(P(("dp", "seq"), "head"), P(("dp", "seq"), None, "head")),
        check_vma=False,
    )
```

```python
import math

import jax
import jax.numpy as jnp
from jax import lax
from jax.experimental import pallas as pl
from jax.experimental.pallas import tpu as pltpu
from jax.sharding import PartitionSpec as P


D = 2048
HEADS = 16
NY = 4
CAP = 2


SMEM = pl.BlockSpec(memory_space=pltpu.SMEM)
VMEM = pl.BlockSpec(memory_space=pltpu.VMEM)
ANY = pl.BlockSpec(memory_space=pl.ANY)
BF = jnp.bfloat16
SMALL = pltpu.CompilerParams(vmem_limit_bytes=8 << 20)
F32 = jnp.float32

OUT = ((0, 1, 2), (3, 4))
BACK = ((4,), (3, 2), (1, 0))


def planes_of(step, nz):
    if step == 0 or 2 * step == nz:
        return (step,)
    return (step, nz - step)


def slots_of(phase, nz):
    return [(d, s) for step in phase for d in planes_of(step, nz) for s in range(CAP)]


def ring(seq, dz, dy):
    nz = seq // NY
    pairs = []
    for z in range(nz):
        for y in range(NY):
            pairs.append((z * NY + y, ((z + dz) % nz) * NY + (y + dy) % NY))
    return pairs


def pick_rows(table, place, blocks, phase, nz):
    slots = slots_of(phase, nz)
    flat, where = [], {}
    for d, pieces in blocks.items():
        where[d] = []
        start = 0
        for a in pieces:
            where[d].append((len(flat), start, a.shape[0]))
            start += a.shape[0]
            flat.append(a)
    tail = flat[0].shape[1:]

    def body(t_ref, p_ref, *refs):
        ins, outs = refs[: len(flat)], refs[len(flat) :]
        for j in range(NY):
            for k, (d, s) in enumerate(slots):
                row = jnp.maximum(t_ref[j, (p_ref[0] + d) % nz * CAP + s], 0)
                if len(where[d]) == 1:
                    outs[j][k] = ins[where[d][0][0]][row]
                    continue
                for n, start, size in where[d]:

                    @pl.when((row >= start) & (row < start + size))
                    def _():
                        outs[j][k] = ins[n][jnp.clip(row - start, 0, size - 1)]

    return pl.pallas_call(
        body,
        in_specs=[SMEM, SMEM] + [VMEM] * len(flat),
        out_specs=[VMEM] * NY,
        out_shape=[jax.ShapeDtypeStruct((len(slots),) + tail, BF)] * NY,
        name="pick",
        compiler_params=SMALL,
    )(table, place, *flat)


def compact(ref_of, place, groups, nz, ref_count):
    flat = [a for group in groups for a in group]
    tail = flat[0].shape[1:]

    def body(r_ref, p_ref, *refs):
        ins, out = refs[:-1], refs[-1]
        for n, phase in enumerate(OUT):
            for j in range(NY):
                for k, (d, s) in enumerate(slots_of(phase, nz)):
                    r = r_ref[j, (p_ref[0] + d) % nz * CAP + s]

                    @pl.when(r >= 0)
                    def _():
                        out[jnp.maximum(r, 0)] = ins[n * NY + j][k]

    return pl.pallas_call(
        body,
        in_specs=[SMEM, SMEM] + [VMEM] * len(flat),
        out_specs=VMEM,
        out_shape=jax.ShapeDtypeStruct((ref_count,) + tail, BF),
        name="compact",
        compiler_params=SMALL,
    )(ref_of, place, *flat)


def spread(ref_of, place, own, other, phase, nz):
    tail = own.shape[1:]
    slots = slots_of(phase, nz)

    def body(r_ref, p_ref, own_ref, other_ref, *outs):
        for j in range(NY):
            for k, (d, s) in enumerate(slots):
                r = r_ref[j, (p_ref[0] + d) % nz * CAP + s]

                @pl.when(r >= 0)
                def _():
                    at = jnp.maximum(r, 0)
                    total = own_ref[at] + other_ref[at].astype(F32)
                    outs[j][k] = total.astype(BF)

    return pl.pallas_call(
        body,
        in_specs=[SMEM, SMEM, VMEM, VMEM],
        out_specs=[VMEM] * NY,
        out_shape=[jax.ShapeDtypeStruct((len(slots),) + tail, BF)] * NY,
        compiler_params=SMALL,
        name="spread",
    )(ref_of, place, own, other)


def gather_grads(table, place, parts, phase, before, step, nz, rows_here):
    planes = planes_of(step, nz)
    tail = parts[0].shape[1:]
    cut = rows_here // 2
    far = 2 * step == nz
    slots = slots_of(phase, nz)
    if far:
        shapes = [(cut,) + tail, (rows_here - cut,) + tail]
    else:
        shapes = [(rows_here,) + tail] * len(planes)
    halves = bool(before) and before[0].shape[0] != rows_here

    def body(t_ref, p_ref, *refs):
        ins = refs[:NY]
        prev = refs[NY : NY + len(before)]
        outs = refs[NY + len(before) : -1]
        acc = refs[-1]

        def fill(r, carry):
            for p in range(len(planes)):
                if step == 0:
                    acc[p, r] = prev[0][r].astype(F32) + prev[1][r].astype(F32)
                elif before and not halves:
                    acc[p, r] = prev[p][r].astype(F32)
                else:
                    acc[p, r] = jnp.zeros(tail, F32)
            return carry

        def low(r, carry):
            acc[0, r] = prev[0][r].astype(F32)
            return carry

        def high(r, carry):
            acc[1, r + cut] = prev[1][r].astype(F32)
            return carry

        lax.fori_loop(0, rows_here, fill, 0)
        if halves:
            lax.fori_loop(0, cut, low, 0)
            lax.fori_loop(0, rows_here - cut, high, 0)
        for p, d in enumerate(planes):
            at_plane = (p_ref[0] + d) % nz * CAP
            for j in range(NY):
                for s in range(CAP):
                    row = t_ref[j, at_plane + s]
                    k = slots.index((d, s))

                    @pl.when(row >= 0)
                    def _():
                        at = jnp.maximum(row, 0)
                        acc[p, at] = acc[p, at] + ins[j][k].astype(F32)

        def drain(r, carry):
            for p in range(len(planes)):
                outs[p][r] = acc[p, r].astype(BF)
            return carry

        def drain_low(r, carry):
            outs[0][r] = acc[0, r].astype(BF)
            return carry

        def drain_high(r, carry):
            outs[1][r] = acc[0, r + cut].astype(BF)
            return carry

        if far:
            lax.fori_loop(0, cut, drain_low, 0)
            lax.fori_loop(0, rows_here - cut, drain_high, 0)
        else:
            lax.fori_loop(0, rows_here, drain, 0)

    return pl.pallas_call(
        body,
        in_specs=[SMEM, SMEM] + [VMEM] * (NY + len(before)),
        out_specs=[VMEM] * len(shapes),
        out_shape=[jax.ShapeDtypeStruct(s, BF) for s in shapes],
        scratch_shapes=[pltpu.VMEM((len(planes), rows_here) + tail, F32)],
        compiler_params=SMALL,
        name="gather",
    )(table, place, *parts, *before)


def fetch(*arrays):
    count = len(arrays)

    def body(*refs):
        sem = refs[-1]
        copies = [
            pltpu.make_async_copy(refs[n], refs[count + n], sem.at[n]) for n in range(count)
        ]
        for copy in copies:
            copy.start()
        for copy in copies:
            copy.wait()

    return pl.pallas_call(
        body,
        in_specs=[pl.BlockSpec(memory_space=pltpu.HBM)] * count,
        out_specs=[VMEM] * count,
        out_shape=[pltpu.VMEM(a.shape, a.dtype) for a in arrays],
        scratch_shapes=[pltpu.SemaphoreType.DMA((count,))],
        compiler_params=SMALL,
        name="fetch",
    )(*arrays)


def core_step(place, own, other, key_weight, value_weight, queries, out_grad, spans, head_size):
    rows, half = own.shape
    tok = queries.shape[0] // spans
    per = rows // spans
    heads = half // head_size
    scaling = 1.0 / math.sqrt(head_size)
    nt = (((1,), (1,)), ((), ()))
    tn = (((0,), (0,)), ((), ()))
    cols = [slice(n * head_size, (n + 1) * head_size) for n in range(heads)]

    def body(
        p_ref, own_ref, oth_ref, wk_ref, wv_ref, q_ref, g_ref, dq_hbm, pown_ref, poth_ref,
        dq_ref, k_ref, v_ref, dk_ref, dv_ref, sem,
    ):
        mine = pl.ds(pl.multiple_of(p_ref[2] * half, half), half)
        theirs = pl.ds(pl.multiple_of((1 - p_ref[2]) * half, half), half)
        for w_ref, out in ((wk_ref, k_ref), (wv_ref, v_ref)):
            total = jnp.dot(own_ref[...], w_ref[mine, :], preferred_element_type=F32)
            total += jnp.dot(oth_ref[...], w_ref[theirs, :], preferred_element_type=F32)
            out[...] = total.astype(BF)

        def span(u, carry):
            here = pl.ds(pl.multiple_of(u * per, per), per)
            there = pl.ds(pl.multiple_of(u * tok, tok), tok)
            q = [q_ref[there, c] for c in cols]
            g = [g_ref[there, c] for c in cols]
            k = [k_ref[here, c] for c in cols]
            v = [v_ref[here, c] for c in cols]
            scores = [
                lax.dot_general(a, b, nt, preferred_element_type=F32) for a, b in zip(k, q)
            ]
            dprobs = [
                lax.dot_general(a, b, nt, preferred_element_type=F32) for a, b in zip(v, g)
            ]
            probs_b, ds = [], []
            for sc, dp in zip(scores, dprobs):
                sc = sc * scaling
                raised = jnp.exp(sc - jnp.max(sc, axis=0, keepdims=True))
                probs = raised / jnp.sum(raised, axis=0, keepdims=True)
                pb = probs.astype(BF)
                delta = jnp.sum(pb.astype(F32) * dp, axis=0, keepdims=True)
                probs_b.append(pb)
                ds.append((probs * (dp - delta)).astype(BF))
            for n, c in enumerate(cols):
                dk = jnp.dot(ds[n], q[n], preferred_element_type=F32) * scaling
                dv = jnp.dot(probs_b[n], g[n], preferred_element_type=F32)
                dq = lax.dot_general(ds[n], k[n], tn, preferred_element_type=F32) * scaling
                dk_ref[here, c] = dk.astype(BF)
                dv_ref[here, c] = dv.astype(BF)
                dq_ref[there, c] = dq.astype(BF)
            return carry

        lax.fori_loop(0, spans, span, 0)
        store = pltpu.make_async_copy(dq_ref, dq_hbm, sem.at[0])
        store.start()
        for at, out in ((theirs, poth_ref), (mine, pown_ref)):
            total = lax.dot_general(dk_ref[...], wk_ref[at, :], nt, preferred_element_type=F32)
            total += lax.dot_general(dv_ref[...], wv_ref[at, :], nt, preferred_element_type=F32)
            out[...] = total.astype(out.dtype)
        store.wait()

    return pl.pallas_call(
        body,
        in_specs=[SMEM, VMEM, VMEM, VMEM, VMEM, VMEM, VMEM],
        out_specs=[ANY, VMEM, VMEM],
        compiler_params=pltpu.CompilerParams(vmem_limit_bytes=16 << 20),
        out_shape=[
            jax.ShapeDtypeStruct(queries.shape, BF),
            jax.ShapeDtypeStruct((rows, half), F32),
            jax.ShapeDtypeStruct((rows, half), BF),
        ],
        scratch_shapes=[pltpu.VMEM(queries.shape, BF)]
        + [pltpu.VMEM((rows, half), BF)] * 4
        + [pltpu.SemaphoreType.DMA((1,))],
        name="core_step",
    )(place, own, other, key_weight, value_weight, queries, out_grad)


def slot_tables(ids, y0, nz, rows_here):
    count = ids.shape[1]
    owner = ids // rows_here
    local = ids % rows_here
    plane = owner // NY
    column = owner % NY
    refs = jnp.arange(count, dtype=jnp.int32)
    same = (owner[:, :, None] == owner[:, None, :]) & (refs[None, None, :] < refs[None, :, None])
    rank = jnp.sum(same.astype(jnp.int32), axis=2)
    code = plane * CAP + rank
    slots = jnp.arange(nz * CAP, dtype=jnp.int32)
    hit = (slots[None, :, None] == code[:, None, :]) & (column == y0)[:, None, :]
    table = jnp.sum(jnp.where(hit, local[:, None, :] + 1, 0), axis=2) - 1
    back = (y0 - column[0]) % NY
    sides = jnp.arange(NY, dtype=jnp.int32)
    mine = (slots[None, :, None] == code[0][None, None, :]) & (
        sides[:, None, None] == back[None, None, :]
    )
    ref_of = jnp.sum(jnp.where(mine, refs[None, None, :] + 1, 0), axis=2) - 1
    return table, ref_of


def whole_step(queries, out_grad, encodings, key_weight, value_weight, neighbours):
    seq = lax.axis_size("seq")
    nz = seq // NY
    far = nz // 2
    index = lax.axis_index("seq")
    head = lax.axis_index("head").astype(jnp.int32)
    z0 = index // NY
    y0 = index % NY
    spans = neighbours.shape[0]
    ref_count = 2 * spans
    rows_here, length, half = encodings.shape
    cut = rows_here // 2

    def move(x, dz, dy):
        return lax.ppermute(x, "seq", ring(seq, dz, dy))

    def swap(x):
        return lax.ppermute(x, "head", [(0, 1), (1, 0)])

    place = jnp.stack([z0, y0, head]).astype(jnp.int32)

    blocks = {0: [encodings]}
    ahead = behind = encodings
    readers = None
    for step in range(1, far + 1):
        if step == far:
            ahead, behind = ahead[cut:], behind[:cut]
        behind = move(behind, 1, 0)
        ahead = move(ahead, -1, 0)
        if step == far:
            blocks[far] = [behind, ahead]
        else:
            blocks[step], blocks[nz - step] = [ahead], [behind]
        if readers is None:
            ids = neighbours.reshape(1, ref_count)
            readers = [ids] + [move(ids, 0, -j) for j in range(1, NY)]
            table, ref_of = slot_tables(jnp.concatenate(readers, axis=0), y0, nz, rows_here)
    groups = []
    for phase in OUT:
        need = {d: blocks[d] for step in phase for d in planes_of(step, nz)}
        picked = pick_rows(table, place, need, phase, nz)
        groups.append([picked[0]] + [move(picked[j], 0, j) for j in range(1, NY)])

    own = compact(ref_of, place, groups, nz, ref_count)
    other = swap(own)
    flat = (ref_count * length, half)
    key_weight, value_weight, queries, out_grad = (
        pltpu.with_memory_space_constraint(a, pltpu.VMEM)
        for a in fetch(
            *(
                pltpu.with_memory_space_constraint(a, pltpu.HBM)
                for a in (key_weight, value_weight, queries, out_grad)
            )
        )
    )
    query_grad, partial_own, partial_other = core_step(
        place, own.reshape(flat), other.reshape(flat), key_weight, value_weight,
        queries, out_grad, spans, D // HEADS,
    )
    came = swap(partial_other)
    shape = (ref_count, length, half)
    partial_own, came = partial_own.reshape(shape), came.reshape(shape)

    before = ()
    for phase in BACK:
        parts = spread(ref_of, place, partial_own, came, phase, nz)
        parts = [parts[0]] + [move(parts[j], 0, -j) for j in range(1, NY)]
        for step in phase:
            total = gather_grads(table, place, parts, phase, before, step, nz, rows_here)
            if step > 0:
                before = (move(total[0], 1, 0), move(total[1], -1, 0))
    return (query_grad, total[0])


def solution(mesh):
    return jax.shard_map(
        whole_step,
        mesh=mesh,
        in_specs=(
            P(("dp", "seq"), "head"),
            P(("dp", "seq"), "head"),
            P(("dp", "seq"), None, "head"),
            P(None, "head"),
            P(None, "head"),
            P(("dp", "seq"), None),
        ),
        out_specs=(P(("dp", "seq"), "head"), P(("dp", "seq"), None, "head")),
        check_vma=False,
    )
```

```python
import math

import jax
import jax.numpy as jnp
from jax import lax
from jax.experimental import pallas as pl
from jax.experimental.pallas import tpu as pltpu
from jax.sharding import PartitionSpec as P


D = 2048
HEADS = 16
NY = 4
CAP = 2


SMEM = pl.BlockSpec(memory_space=pltpu.SMEM)
VMEM = pl.BlockSpec(memory_space=pltpu.VMEM)
ANY = pl.BlockSpec(memory_space=pl.ANY)
BF = jnp.bfloat16
SMALL = pltpu.CompilerParams(vmem_limit_bytes=8 << 20)
F32 = jnp.float32

OUT = ((0, 1, 2), (3, 4))
BACK = ((4,), (3,), (2,), (1, 0))


def planes_of(step, nz):
    if step == 0 or 2 * step == nz:
        return (step,)
    return (step, nz - step)


def span_of(phase, nz):
    planes = sorted((d + nz // 2 - 1) % nz - (nz // 2 - 1) for t in phase for d in planes_of(t, nz))
    if nz // 2 - 1 in planes or nz // 2 in planes:
        planes = sorted(d % nz for d in planes)
    stride = planes[1] - planes[0] if len(planes) > 1 else 1
    assert planes == [planes[0] + stride * n for n in range(len(planes))]
    return planes[0], stride, len(planes)


def slots_of(phase, nz):
    first, stride, count = span_of(phase, nz)
    return [((first + stride * n) % nz, s) for n in range(count) for s in range(CAP)]


def ring(seq, dz, dy):
    nz = seq // NY
    pairs = []
    for z in range(nz):
        for y in range(NY):
            pairs.append((z * NY + y, ((z + dz) % nz) * NY + (y + dy) % NY))
    return pairs


def pick_rows(table, place, blocks, phase, nz):
    slots = slots_of(phase, nz)
    flat, where = [], {}
    for d, pieces in blocks.items():
        where[d] = []
        start = 0
        for a in pieces:
            where[d].append((len(flat), start, a.shape[0]))
            start += a.shape[0]
            flat.append(a)
    tail = flat[0].shape[1:]

    def body(t_ref, p_ref, *refs):
        ins, outs = refs[: len(flat)], refs[len(flat) :]
        for j in range(NY):
            for k, (d, s) in enumerate(slots):
                row = jnp.maximum(t_ref[j, (p_ref[0] + d) % nz * CAP + s], 0)
                if len(where[d]) == 1:
                    outs[j][k] = ins[where[d][0][0]][row]
                    continue
                for n, start, size in where[d]:

                    @pl.when((row >= start) & (row < start + size))
                    def _():
                        outs[j][k] = ins[n][jnp.clip(row - start, 0, size - 1)]

    return pl.pallas_call(
        body,
        in_specs=[SMEM, SMEM] + [VMEM] * len(flat),
        out_specs=[VMEM] * NY,
        out_shape=[jax.ShapeDtypeStruct((len(slots),) + tail, BF)] * NY,
        name="pick",
        compiler_params=SMALL,
    )(table, place, *flat)


def compact(ref_of, place, groups, nz, ref_count):
    flat = [a for group in groups for a in group]
    tail = flat[0].shape[1:]

    def body(r_ref, p_ref, *refs):
        ins, out = refs[:-1], refs[-1]
        for n, phase in enumerate(OUT):
            first, stride, count = span_of(phase, nz)
            for j in range(NY):

                def place_one(k, carry):
                    plane = (p_ref[0] + nz + first + stride * (k // CAP)) % nz
                    r = r_ref[j, plane * CAP + k % CAP]

                    @pl.when(r >= 0)
                    def _():
                        out[jnp.maximum(r, 0)] = ins[n * NY + j][k]

                    return carry

                lax.fori_loop(0, count * CAP, place_one, 0, unroll=2)

    return pl.pallas_call(
        body,
        in_specs=[SMEM, SMEM] + [VMEM] * len(flat),
        out_specs=VMEM,
        out_shape=jax.ShapeDtypeStruct((ref_count,) + tail, BF),
        name="compact",
        compiler_params=SMALL,
    )(ref_of, place, *flat)


def spread(ref_of, place, own, other, phase, nz):
    tail = own.shape[1:]
    slots = slots_of(phase, nz)
    first, stride, _ = span_of(phase, nz)

    def body(r_ref, p_ref, own_ref, other_ref, *outs):
        for j in range(NY):

            def place_one(k, carry):
                plane = (p_ref[0] + nz + first + stride * (k // CAP)) % nz
                r = r_ref[j, plane * CAP + k % CAP]

                @pl.when(r >= 0)
                def _():
                    at = jnp.maximum(r, 0)
                    total = own_ref[at] + other_ref[at].astype(F32)
                    outs[j][k] = total.astype(BF)

                return carry

            lax.fori_loop(0, len(slots), place_one, 0, unroll=2)

    return pl.pallas_call(
        body,
        in_specs=[SMEM, SMEM, VMEM, VMEM],
        out_specs=[VMEM] * NY,
        out_shape=[jax.ShapeDtypeStruct((len(slots),) + tail, BF)] * NY,
        compiler_params=SMALL,
        name="spread",
    )(ref_of, place, own, other)


def gather_grads(table, place, parts, phase, before, step, nz, rows_here):
    planes = planes_of(step, nz)
    tail = parts[0].shape[1:]
    cut = rows_here // 2
    far = 2 * step == nz
    slots = slots_of(phase, nz)
    if far:
        shapes = [(cut,) + tail, (rows_here - cut,) + tail]
    else:
        shapes = [(rows_here,) + tail] * len(planes)
    halves = bool(before) and before[0].shape[0] != rows_here

    def body(t_ref, p_ref, *refs):
        ins = refs[:NY]
        prev = refs[NY : NY + len(before)]
        outs = refs[NY + len(before) : -1]
        acc = refs[-1]

        def fill(r, carry):
            for p in range(len(planes)):
                if step == 0:
                    acc[p, r] = prev[0][r].astype(F32) + prev[1][r].astype(F32)
                elif before and not halves:
                    acc[p, r] = prev[p][r].astype(F32)
                else:
                    acc[p, r] = jnp.zeros(tail, F32)
            return carry

        def low(r, carry):
            acc[0, r] = prev[0][r].astype(F32)
            return carry

        def high(r, carry):
            acc[1, r + cut] = prev[1][r].astype(F32)
            return carry

        lax.fori_loop(0, rows_here, fill, 0)
        if halves:
            lax.fori_loop(0, cut, low, 0)
            lax.fori_loop(0, rows_here - cut, high, 0)
        for p, d in enumerate(planes):
            at_plane = (p_ref[0] + d) % nz * CAP
            for j in range(NY):
                for s in range(CAP):
                    row = t_ref[j, at_plane + s]
                    k = slots.index((d, s))

                    @pl.when(row >= 0)
                    def _():
                        at = jnp.maximum(row, 0)
                        acc[p, at] = acc[p, at] + ins[j][k].astype(F32)

        def drain(r, carry):
            for p in range(len(planes)):
                outs[p][r] = acc[p, r].astype(BF)
            return carry

        def drain_low(r, carry):
            outs[0][r] = acc[0, r].astype(BF)
            return carry

        def drain_high(r, carry):
            outs[1][r] = acc[0, r + cut].astype(BF)
            return carry

        if far:
            lax.fori_loop(0, cut, drain_low, 0)
            lax.fori_loop(0, rows_here - cut, drain_high, 0)
        else:
            lax.fori_loop(0, rows_here, drain, 0)

    return pl.pallas_call(
        body,
        in_specs=[SMEM, SMEM] + [VMEM] * (NY + len(before)),
        out_specs=[VMEM] * len(shapes),
        out_shape=[jax.ShapeDtypeStruct(s, BF) for s in shapes],
        scratch_shapes=[pltpu.VMEM((len(planes), rows_here) + tail, F32)],
        compiler_params=SMALL,
        name="gather",
    )(table, place, *parts, *before)


def fetch(*arrays):
    count = len(arrays)

    def body(*refs):
        sem = refs[-1]
        copies = [
            pltpu.make_async_copy(refs[n], refs[count + n], sem.at[n]) for n in range(count)
        ]
        for copy in copies:
            copy.start()
        for copy in copies:
            copy.wait()

    return pl.pallas_call(
        body,
        in_specs=[pl.BlockSpec(memory_space=pltpu.HBM)] * count,
        out_specs=[VMEM] * count,
        out_shape=[pltpu.VMEM(a.shape, a.dtype) for a in arrays],
        scratch_shapes=[pltpu.SemaphoreType.DMA((count,))],
        compiler_params=SMALL,
        name="fetch",
    )(*arrays)


def project_own(place, own, key_weight, value_weight):
    rows, half = own.shape

    def body(p_ref, own_ref, wk_ref, wv_ref, k_ref, v_ref):
        mine = pl.ds(pl.multiple_of(p_ref[2] * half, half), half)
        for w_ref, out in ((wk_ref, k_ref), (wv_ref, v_ref)):
            out[...] = jnp.dot(own_ref[...], w_ref[mine, :], preferred_element_type=F32)

    return pl.pallas_call(
        body,
        in_specs=[SMEM] + [VMEM] * 3,
        out_specs=[VMEM] * 2,
        out_shape=[jax.ShapeDtypeStruct((rows, half), F32)] * 2,
        compiler_params=SMALL,
        name="project_own",
    )(place, own, key_weight, value_weight)


def return_own(place, key_grad, value_grad, key_weight, value_weight):
    rows, half = key_grad.shape
    nt = (((1,), (1,)), ((), ()))

    def body(p_ref, dk_ref, dv_ref, wk_ref, wv_ref, out):
        mine = pl.ds(pl.multiple_of(p_ref[2] * half, half), half)
        total = lax.dot_general(dk_ref[...], wk_ref[mine, :], nt, preferred_element_type=F32)
        total += lax.dot_general(dv_ref[...], wv_ref[mine, :], nt, preferred_element_type=F32)
        out[...] = total

    return pl.pallas_call(
        body,
        in_specs=[SMEM] + [VMEM] * 4,
        out_specs=VMEM,
        out_shape=jax.ShapeDtypeStruct((rows, half), F32),
        compiler_params=SMALL,
        name="return_own",
    )(place, key_grad, value_grad, key_weight, value_weight)


def core_step(
    place, key_part, value_part, other, key_weight, value_weight, queries, out_grad, spans, head_size
):
    rows, half = other.shape
    tok = queries.shape[0] // spans
    per = rows // spans
    heads = half // head_size
    scaling = 1.0 / math.sqrt(head_size)
    nt = (((1,), (1,)), ((), ()))
    tn = (((0,), (0,)), ((), ()))
    cols = [slice(n * head_size, (n + 1) * head_size) for n in range(heads)]

    def body(
        p_ref, ka_ref, va_ref, oth_ref, wk_ref, wv_ref, q_ref, g_ref,
        dq_hbm, poth_ref, dk_ref, dv_ref, dq_ref, k_ref, v_ref, sem,
    ):
        theirs = pl.ds(pl.multiple_of((1 - p_ref[2]) * half, half), half)
        for part, w_ref, out in ((ka_ref, wk_ref, k_ref), (va_ref, wv_ref, v_ref)):
            total = jnp.dot(oth_ref[...], w_ref[theirs, :], preferred_element_type=F32)
            out[...] = (part[...] + total).astype(BF)

        def at(u):
            return (
                pl.ds(pl.multiple_of(u * per, per), per),
                pl.ds(pl.multiple_of(u * tok, tok), tok),
            )

        def weigh(u):
            here, there = at(u)
            probs_b, ds = [], []
            scores = [
                lax.dot_general(k_ref[here, c], q_ref[there, c], nt, preferred_element_type=F32)
                for c in cols
            ]
            dprobs = [
                lax.dot_general(v_ref[here, c], g_ref[there, c], nt, preferred_element_type=F32)
                for c in cols
            ]
            for sc, dp in zip(scores, dprobs):
                sc = sc * scaling
                raised = jnp.exp(sc - jnp.max(sc, axis=0, keepdims=True))
                probs = raised / jnp.sum(raised, axis=0, keepdims=True)
                pb = probs.astype(BF)
                delta = jnp.sum(pb.astype(F32) * dp, axis=0, keepdims=True)
                probs_b.append(pb)
                ds.append((probs * (dp - delta)).astype(BF))
            return tuple(probs_b), tuple(ds)

        def grads(u, probs_b, ds):
            here, there = at(u)
            for n, c in enumerate(cols):
                q, g, k = q_ref[there, c], g_ref[there, c], k_ref[here, c]
                dk = jnp.dot(ds[n], q, preferred_element_type=F32) * scaling
                dv = jnp.dot(probs_b[n], g, preferred_element_type=F32)
                dq = lax.dot_general(ds[n], k, tn, preferred_element_type=F32) * scaling
                dk_ref[here, c] = dk.astype(BF)
                dv_ref[here, c] = dv.astype(BF)
                dq_ref[there, c] = dq.astype(BF)

        def both(u, carry):
            after = weigh(u + 1)
            grads(u, *carry)
            return after

        grads(spans - 1, *lax.fori_loop(0, spans - 1, both, weigh(0)))
        store = pltpu.make_async_copy(dq_ref, dq_hbm, sem.at[0])
        store.start()
        total = lax.dot_general(dk_ref[...], wk_ref[theirs, :], nt, preferred_element_type=F32)
        total += lax.dot_general(dv_ref[...], wv_ref[theirs, :], nt, preferred_element_type=F32)
        poth_ref[...] = total.astype(BF)
        store.wait()

    return pl.pallas_call(
        body,
        in_specs=[SMEM] + [VMEM] * 7,
        out_specs=[ANY] + [VMEM] * 3,
        compiler_params=pltpu.CompilerParams(vmem_limit_bytes=16 << 20),
        out_shape=[
            jax.ShapeDtypeStruct(queries.shape, BF),
        ]
        + [jax.ShapeDtypeStruct((rows, half), BF)] * 3,
        scratch_shapes=[pltpu.VMEM(queries.shape, BF)]
        + [pltpu.VMEM((rows, half), BF)] * 2
        + [pltpu.SemaphoreType.DMA((1,))],
        name="core_step",
    )(place, key_part, value_part, other, key_weight, value_weight, queries, out_grad)


def slot_tables(ids, y0, nz, rows_here):
    count = ids.shape[1]
    owner = ids // rows_here
    local = ids % rows_here
    plane = owner // NY
    column = owner % NY
    refs = jnp.arange(count, dtype=jnp.int32)
    same = (owner[:, :, None] == owner[:, None, :]) & (refs[None, None, :] < refs[None, :, None])
    rank = jnp.sum(same.astype(jnp.int32), axis=2)
    code = plane * CAP + rank
    slots = jnp.arange(nz * CAP, dtype=jnp.int32)
    hit = (slots[None, :, None] == code[:, None, :]) & (column == y0)[:, None, :]
    table = jnp.sum(jnp.where(hit, local[:, None, :] + 1, 0), axis=2) - 1
    back = (y0 - column[0]) % NY
    sides = jnp.arange(NY, dtype=jnp.int32)
    mine = (slots[None, :, None] == code[0][None, None, :]) & (
        sides[:, None, None] == back[None, None, :]
    )
    ref_of = jnp.sum(jnp.where(mine, refs[None, None, :] + 1, 0), axis=2) - 1
    return table, ref_of


def whole_step(queries, out_grad, encodings, key_weight, value_weight, neighbours):
    seq = lax.axis_size("seq")
    nz = seq // NY
    far = nz // 2
    index = lax.axis_index("seq")
    head = lax.axis_index("head").astype(jnp.int32)
    z0 = index // NY
    y0 = index % NY
    spans = neighbours.shape[0]
    ref_count = 2 * spans
    rows_here, length, half = encodings.shape
    cut = rows_here // 2

    def move(x, dz, dy):
        return lax.ppermute(x, "seq", ring(seq, dz, dy))

    def swap(x):
        return lax.ppermute(x, "head", [(0, 1), (1, 0)])

    place = jnp.stack([z0, y0, head]).astype(jnp.int32)

    blocks = {0: [encodings]}
    ahead = behind = encodings
    readers = None
    for step in range(1, far + 1):
        if step == far:
            ahead, behind = lax.optimization_barrier((ahead[cut:], behind[:cut]))
        behind = move(behind, 1, 0)
        ahead = move(ahead, -1, 0)
        if step == far:
            blocks[far] = [behind, ahead]
        else:
            blocks[step], blocks[nz - step] = [ahead], [behind]
        if readers is None:
            ids = neighbours.reshape(1, ref_count)
            two = jnp.concatenate([ids, move(ids, 0, -1)], axis=0)
            readers = jnp.concatenate([two, move(two, 0, -2)], axis=0)
            table, ref_of = slot_tables(readers, y0, nz, rows_here)
    groups = []
    for phase in OUT:
        need = {d: blocks[d] for step in phase for d in planes_of(step, nz)}
        picked = pick_rows(table, place, need, phase, nz)
        groups.append([picked[0]] + [move(picked[j], 0, j) for j in range(1, NY)])

    key_weight, value_weight, queries, out_grad = (
        pltpu.with_memory_space_constraint(a, pltpu.VMEM)
        for a in fetch(
            *(
                pltpu.with_memory_space_constraint(a, pltpu.HBM)
                for a in (key_weight, value_weight, queries, out_grad)
            )
        )
    )
    flat = (ref_count * length, half)
    own = compact(ref_of, place, groups, nz, ref_count)
    other = swap(own)
    parts = project_own(place, own.reshape(flat), key_weight, value_weight)
    query_grad, partial_other, key_grad, value_grad = core_step(
        place, *parts, other.reshape(flat), key_weight, value_weight, queries, out_grad,
        spans, D // HEADS,
    )
    came = swap(partial_other)
    partial_own = return_own(place, key_grad, value_grad, key_weight, value_weight)
    shape = (ref_count, length, half)
    partial_own, came = partial_own.reshape(shape), came.reshape(shape)

    before = ()
    for phase in BACK:
        parts = spread(ref_of, place, partial_own, came, phase, nz)
        parts = [parts[0]] + [move(parts[j], 0, -j) for j in range(1, NY)]
        for step in phase:
            total = gather_grads(table, place, parts, phase, before, step, nz, rows_here)
            if step > 0:
                before = (move(total[0], 1, 0), move(total[1], -1, 0))
    return (query_grad, total[0])


def solution(mesh):
    return jax.shard_map(
        whole_step,
        mesh=mesh,
        in_specs=(
            P(("dp", "seq"), "head"),
            P(("dp", "seq"), "head"),
            P(("dp", "seq"), None, "head"),
            P(None, "head"),
            P(None, "head"),
            P(("dp", "seq"), None),
        ),
        out_specs=(P(("dp", "seq"), "head"), P(("dp", "seq"), None, "head")),
        check_vma=False,
    )
```

```python
import math

import jax
import jax.numpy as jnp
from jax import lax
from jax.experimental import pallas as pl
from jax.experimental.pallas import tpu as pltpu
from jax.sharding import PartitionSpec as P


D = 2048
HEADS = 16
NY = 4
CAP = 2
SPARE = 2
WIDE = 512


SMEM = pl.BlockSpec(memory_space=pltpu.SMEM)
VMEM = pl.BlockSpec(memory_space=pltpu.VMEM)
ANY = pl.BlockSpec(memory_space=pl.ANY)
BF = jnp.bfloat16
SMALL = pltpu.CompilerParams(vmem_limit_bytes=8 << 20)
F32 = jnp.float32

OUT = ((0, 1, 2), (3, 4))
BACK = ((4,), (3,), (2,), (1, 0))


def planes_of(step, nz):
    if step == 0 or 2 * step == nz:
        return (step,)
    return (step, nz - step)


def span_of(phase, nz):
    planes = sorted((d + nz // 2 - 1) % nz - (nz // 2 - 1) for t in phase for d in planes_of(t, nz))
    if nz // 2 - 1 in planes or nz // 2 in planes:
        planes = sorted(d % nz for d in planes)
    stride = planes[1] - planes[0] if len(planes) > 1 else 1
    assert planes == [planes[0] + stride * n for n in range(len(planes))]
    return planes[0], stride, len(planes)


def slots_of(phase, nz):
    first, stride, count = span_of(phase, nz)
    return [((first + stride * n) % nz, s) for n in range(count) for s in range(CAP)]


def ring(seq, dz, dy):
    nz = seq // NY
    pairs = []
    for z in range(nz):
        for y in range(NY):
            pairs.append((z * NY + y, ((z + dz) % nz) * NY + (y + dy) % NY))
    return pairs


def pick_rows(table, place, blocks, phase, nz):
    slots = slots_of(phase, nz)
    flat, where = [], {}
    for d, pieces in blocks.items():
        where[d] = []
        start = 0
        for a in pieces:
            where[d].append((len(flat), start, a.shape[0]))
            start += a.shape[0]
            flat.append(a)
    tail = flat[0].shape[1:]

    def body(t_ref, p_ref, *refs):
        ins, outs = refs[: len(flat)], refs[len(flat) :]
        for j in range(NY):
            for k, (d, s) in enumerate(slots):
                row = jnp.maximum(t_ref[j, (p_ref[0] + d) % nz * CAP + s], 0)
                if len(where[d]) == 1:
                    outs[j][k] = ins[where[d][0][0]][row]
                    continue
                for n, start, size in where[d]:

                    @pl.when((row >= start) & (row < start + size))
                    def _():
                        outs[j][k] = ins[n][jnp.clip(row - start, 0, size - 1)]

    return pl.pallas_call(
        body,
        in_specs=[SMEM, SMEM] + [VMEM] * len(flat),
        out_specs=[VMEM] * NY,
        out_shape=[jax.ShapeDtypeStruct((len(slots),) + tail, BF)] * NY,
        name="pick",
        compiler_params=SMALL,
    )(table, place, *flat)


def compact(ref_of, place, groups, nz, ref_count):
    flat = [a for group in groups for a in group]
    tail = flat[0].shape[1:]

    def body(r_ref, p_ref, *refs):
        ins, out = refs[:-1], refs[-1]
        for n, phase in enumerate(OUT):
            first, stride, count = span_of(phase, nz)

            def place_slots(k, carry):
                plane = (p_ref[0] + nz + first + stride * (k // CAP)) % nz
                at = [r_ref[j, plane * CAP + k % CAP] for j in range(NY)]
                for j in range(NY):
                    out[jnp.where(at[j] < 0, ref_count, at[j])] = ins[n * NY + j][k]
                return carry

            lax.fori_loop(0, count * CAP, place_slots, 0)

    return pl.pallas_call(
        body,
        in_specs=[SMEM, SMEM] + [VMEM] * len(flat),
        out_specs=VMEM,
        out_shape=jax.ShapeDtypeStruct((ref_count + SPARE,) + tail, BF),
        name="compact",
        compiler_params=SMALL,
    )(ref_of, place, *flat)


def spread(ref_of, place, own, other, phase, nz):
    tail = own.shape[1:]
    slots = slots_of(phase, nz)
    first, stride, _ = span_of(phase, nz)

    def body(r_ref, p_ref, own_ref, other_ref, *outs):
        def place_slots(k, carry):
            plane = (p_ref[0] + nz + first + stride * (k // CAP)) % nz
            at = [jnp.maximum(r_ref[j, plane * CAP + k % CAP], 0) for j in range(NY)]
            for j in range(NY):
                total = own_ref[at[j]] + other_ref[at[j]].astype(F32)
                outs[j][k] = total.astype(BF)
            return carry

        lax.fori_loop(0, len(slots), place_slots, 0)

    return pl.pallas_call(
        body,
        in_specs=[SMEM, SMEM, VMEM, VMEM],
        out_specs=[VMEM] * NY,
        out_shape=[jax.ShapeDtypeStruct((len(slots),) + tail, BF)] * NY,
        compiler_params=SMALL,
        name="spread",
    )(ref_of, place, own, other)


def gather_grads(table, place, parts, phase, before, step, nz, rows_here):
    planes = planes_of(step, nz)
    tail = parts[0].shape[1:]
    cut = rows_here // 2
    far = 2 * step == nz
    slots = slots_of(phase, nz)
    if far:
        shapes = [(cut,) + tail, (rows_here - cut,) + tail]
    else:
        shapes = [(rows_here,) + tail] * len(planes)
    halves = bool(before) and before[0].shape[0] != rows_here

    def body(t_ref, p_ref, *refs):
        ins = refs[:NY]
        prev = refs[NY : NY + len(before)]
        outs = refs[NY + len(before) : -1]
        acc = refs[-1]

        def fill(r, carry):
            for p in range(len(planes)):
                if step == 0:
                    acc[p, r] = prev[0][r].astype(F32) + prev[1][r].astype(F32)
                elif before and not halves:
                    acc[p, r] = prev[p][r].astype(F32)
                else:
                    acc[p, r] = jnp.zeros(tail, F32)
            return carry

        def low(r, carry):
            acc[0, r] = prev[0][r].astype(F32)
            return carry

        def high(r, carry):
            acc[1, r + cut] = prev[1][r].astype(F32)
            return carry

        lax.fori_loop(0, rows_here, fill, 0)
        if halves:
            lax.fori_loop(0, cut, low, 0)
            lax.fori_loop(0, rows_here - cut, high, 0)
        for p, d in enumerate(planes):
            at_plane = (p_ref[0] + d) % nz * CAP
            for j in range(NY):
                for s in range(CAP):
                    row = t_ref[j, at_plane + s]
                    k = slots.index((d, s))

                    @pl.when(row >= 0)
                    def _():
                        at = jnp.maximum(row, 0)
                        acc[p, at] = acc[p, at] + ins[j][k].astype(F32)

        def drain(r, carry):
            for p in range(len(planes)):
                outs[p][r] = acc[p, r].astype(BF)
            return carry

        def drain_low(r, carry):
            outs[0][r] = acc[0, r].astype(BF)
            return carry

        def drain_high(r, carry):
            outs[1][r] = acc[0, r + cut].astype(BF)
            return carry

        if far:
            lax.fori_loop(0, cut, drain_low, 0)
            lax.fori_loop(0, rows_here - cut, drain_high, 0)
        else:
            lax.fori_loop(0, rows_here, drain, 0)

    return pl.pallas_call(
        body,
        in_specs=[SMEM, SMEM] + [VMEM] * (NY + len(before)),
        out_specs=[VMEM] * len(shapes),
        out_shape=[jax.ShapeDtypeStruct(s, BF) for s in shapes],
        scratch_shapes=[pltpu.VMEM((len(planes), rows_here) + tail, F32)],
        compiler_params=SMALL,
        name="gather",
    )(table, place, *parts, *before)


def fetch(*arrays):
    count = len(arrays)

    def body(*refs):
        sem = refs[-1]
        copies = [
            pltpu.make_async_copy(refs[n], refs[count + n], sem.at[n]) for n in range(count)
        ]
        for copy in copies:
            copy.start()
        for copy in copies:
            copy.wait()

    return pl.pallas_call(
        body,
        in_specs=[pl.BlockSpec(memory_space=pltpu.HBM)] * count,
        out_specs=[VMEM] * count,
        out_shape=[pltpu.VMEM(a.shape, a.dtype) for a in arrays],
        scratch_shapes=[pltpu.SemaphoreType.DMA((count,))],
        compiler_params=SMALL,
        name="fetch",
    )(*arrays)


def project_own(place, own, key_weight, value_weight, rows):
    half = own.shape[1]

    def body(p_ref, own_ref, wk_ref, wv_ref, k_ref, v_ref):
        mine = pl.ds(pl.multiple_of(p_ref[2] * half, half), half)

        def block(n, carry):
            c = pl.ds(pl.multiple_of(n * WIDE, WIDE), WIDE)
            for w_ref, out in ((wk_ref, k_ref), (wv_ref, v_ref)):
                out[:, c] = jnp.dot(own_ref[:rows], w_ref[mine, c], preferred_element_type=F32)
            return carry

        lax.fori_loop(0, half // WIDE, block, 0)

    return pl.pallas_call(
        body,
        in_specs=[SMEM] + [VMEM] * 3,
        out_specs=[VMEM] * 2,
        out_shape=[jax.ShapeDtypeStruct((rows, half), F32)] * 2,
        compiler_params=SMALL,
        name="project_own",
    )(place, own, key_weight, value_weight)


def return_own(place, key_grad, value_grad, key_weight, value_weight):
    rows, half = key_grad.shape
    nt = (((1,), (1,)), ((), ()))

    def body(p_ref, dk_ref, dv_ref, wk_ref, wv_ref, out):
        def block(n, carry):
            c = pl.ds(pl.multiple_of(n * WIDE, WIDE), WIDE)
            at = pl.ds(pl.multiple_of(p_ref[2] * half + n * WIDE, WIDE), WIDE)
            total = lax.dot_general(dk_ref[...], wk_ref[at, :], nt, preferred_element_type=F32)
            total += lax.dot_general(dv_ref[...], wv_ref[at, :], nt, preferred_element_type=F32)
            out[:, c] = total
            return carry

        lax.fori_loop(0, half // WIDE, block, 0)

    return pl.pallas_call(
        body,
        in_specs=[SMEM] + [VMEM] * 4,
        out_specs=VMEM,
        out_shape=jax.ShapeDtypeStruct((rows, half), F32),
        compiler_params=SMALL,
        name="return_own",
    )(place, key_grad, value_grad, key_weight, value_weight)


def into_vmem(*arrays):
    held = fetch(*(pltpu.with_memory_space_constraint(a, pltpu.HBM) for a in arrays))
    return [pltpu.with_memory_space_constraint(a, pltpu.VMEM) for a in held]


def core_step(
    place, key_part, value_part, other, key_weight, value_weight, queries, out_grad, spans, head_size
):
    rows, half = key_part.shape
    tok = queries.shape[0] // spans
    per = rows // spans
    heads = half // head_size
    scaling = 1.0 / math.sqrt(head_size)
    nt = (((1,), (1,)), ((), ()))
    tn = (((0,), (0,)), ((), ()))
    cols = [slice(n * head_size, (n + 1) * head_size) for n in range(heads)]

    def body(
        p_ref, ka_ref, va_ref, oth_ref, wk_ref, wv_ref, q_ref, g_ref,
        dq_hbm, poth_ref, dk_ref, dv_ref, dq_ref, k_ref, v_ref, sem,
    ):
        theirs = pl.ds(pl.multiple_of((1 - p_ref[2]) * half, half), half)

        def project(n, carry):
            c = pl.ds(pl.multiple_of(n * WIDE, WIDE), WIDE)
            for part, w_ref, out in ((ka_ref, wk_ref, k_ref), (va_ref, wv_ref, v_ref)):
                total = jnp.dot(oth_ref[:rows], w_ref[theirs, c], preferred_element_type=F32)
                out[:, c] = (part[:, c] + total).astype(BF)
            return carry

        lax.fori_loop(0, half // WIDE, project, 0)

        def at(u):
            return (
                pl.ds(pl.multiple_of(u * per, per), per),
                pl.ds(pl.multiple_of(u * tok, tok), tok),
            )

        def weigh(u):
            here, there = at(u)
            probs_b, ds = [], []
            scores = [
                lax.dot_general(k_ref[here, c], q_ref[there, c], nt, preferred_element_type=F32)
                for c in cols
            ]
            dprobs = [
                lax.dot_general(v_ref[here, c], g_ref[there, c], nt, preferred_element_type=F32)
                for c in cols
            ]
            for sc, dp in zip(scores, dprobs):
                sc = sc * scaling
                raised = jnp.exp(sc - jnp.max(sc, axis=0, keepdims=True))
                probs = raised / jnp.sum(raised, axis=0, keepdims=True)
                pb = probs.astype(BF)
                delta = jnp.sum(pb.astype(F32) * dp, axis=0, keepdims=True)
                probs_b.append(pb)
                ds.append((probs * (dp - delta)).astype(BF))
            return tuple(probs_b), tuple(ds)

        def grads(u, probs_b, ds):
            here, there = at(u)
            for n, c in enumerate(cols):
                q, g, k = q_ref[there, c], g_ref[there, c], k_ref[here, c]
                dk = jnp.dot(ds[n], q, preferred_element_type=F32) * scaling
                dv = jnp.dot(probs_b[n], g, preferred_element_type=F32)
                dq = lax.dot_general(ds[n], k, tn, preferred_element_type=F32) * scaling
                dk_ref[here, c] = dk.astype(BF)
                dv_ref[here, c] = dv.astype(BF)
                dq_ref[there, c] = dq.astype(BF)

        def both(u, carry):
            after = weigh(u + 1)
            grads(u, *carry)
            return after

        grads(spans - 1, *lax.fori_loop(0, spans - 1, both, weigh(0)))
        store = pltpu.make_async_copy(dq_ref, dq_hbm, sem.at[0])
        store.start()

        def back(n, carry):
            c = pl.ds(pl.multiple_of(n * WIDE, WIDE), WIDE)
            at_rows = pl.ds(pl.multiple_of((1 - p_ref[2]) * half + n * WIDE, WIDE), WIDE)
            total = lax.dot_general(
                dk_ref[...], wk_ref[at_rows, :], nt, preferred_element_type=F32
            )
            total += lax.dot_general(
                dv_ref[...], wv_ref[at_rows, :], nt, preferred_element_type=F32
            )
            poth_ref[:, c] = total.astype(BF)
            return carry

        lax.fori_loop(0, half // WIDE, back, 0)
        store.wait()

    return pl.pallas_call(
        body,
        in_specs=[SMEM] + [VMEM] * 7,
        out_specs=[ANY] + [VMEM] * 3,
        compiler_params=pltpu.CompilerParams(vmem_limit_bytes=16 << 20),
        out_shape=[
            jax.ShapeDtypeStruct(queries.shape, BF),
        ]
        + [jax.ShapeDtypeStruct((rows, half), BF)] * 3,
        scratch_shapes=[pltpu.VMEM(queries.shape, BF)]
        + [pltpu.VMEM((rows, half), BF)] * 2
        + [pltpu.SemaphoreType.DMA((1,))],
        name="core_step",
    )(place, key_part, value_part, other, key_weight, value_weight, queries, out_grad)


def slot_tables(ids, y0, nz, rows_here):
    count = ids.shape[1]
    owner = ids // rows_here
    local = ids % rows_here
    plane = owner // NY
    column = owner % NY
    refs = jnp.arange(count, dtype=jnp.int32)
    same = (owner[:, :, None] == owner[:, None, :]) & (refs[None, None, :] < refs[None, :, None])
    rank = jnp.sum(same.astype(jnp.int32), axis=2)
    code = plane * CAP + rank
    slots = jnp.arange(nz * CAP, dtype=jnp.int32)
    hit = (slots[None, :, None] == code[:, None, :]) & (column == y0)[:, None, :]
    table = jnp.sum(jnp.where(hit, local[:, None, :] + 1, 0), axis=2) - 1
    back = (y0 - column[0]) % NY
    sides = jnp.arange(NY, dtype=jnp.int32)
    mine = (slots[None, :, None] == code[0][None, None, :]) & (
        sides[:, None, None] == back[None, None, :]
    )
    ref_of = jnp.sum(jnp.where(mine, refs[None, None, :] + 1, 0), axis=2) - 1
    return table, ref_of


def whole_step(queries, out_grad, encodings, key_weight, value_weight, neighbours):
    seq = lax.axis_size("seq")
    nz = seq // NY
    far = nz // 2
    index = lax.axis_index("seq")
    head = lax.axis_index("head").astype(jnp.int32)
    z0 = index // NY
    y0 = index % NY
    spans = neighbours.shape[0]
    ref_count = 2 * spans
    rows_here, length, half = encodings.shape
    cut = rows_here // 2

    def move(x, dz, dy):
        return lax.ppermute(x, "seq", ring(seq, dz, dy))

    def swap(x):
        return lax.ppermute(x, "head", [(0, 1), (1, 0)])

    place = jnp.stack([z0, y0, head]).astype(jnp.int32)

    blocks = {0: into_vmem(encodings)}
    ahead = behind = encodings
    readers = None
    for step in range(1, far + 1):
        if step == far:
            ahead, behind = lax.optimization_barrier((ahead[cut:], behind[:cut]))
        behind = move(behind, 1, 0)
        ahead = move(ahead, -1, 0)
        if step == far:
            blocks[far] = [behind, ahead]
        else:
            blocks[step], blocks[nz - step] = [ahead], [behind]
        if readers is None:
            ids = neighbours.reshape(1, ref_count)
            two = jnp.concatenate([ids, move(ids, 0, -1)], axis=0)
            readers = jnp.concatenate([two, move(two, 0, -2)], axis=0)
            table, ref_of = slot_tables(readers, y0, nz, rows_here)
    groups = []
    for phase in OUT:
        need = {d: blocks[d] for step in phase for d in planes_of(step, nz)}
        picked = pick_rows(table, place, need, phase, nz)
        groups.append([picked[0]] + [move(picked[j], 0, j) for j in range(1, NY)])

    key_weight, value_weight, queries, out_grad = into_vmem(
        key_weight, value_weight, queries, out_grad
    )
    flat = (ref_count * length, half)
    own = compact(ref_of, place, groups, nz, ref_count)
    other = swap(own)
    parts = project_own(place, own.reshape(-1, half), key_weight, value_weight, flat[0])
    query_grad, partial_other, key_grad, value_grad = core_step(
        place, *parts, other.reshape(-1, half), key_weight, value_weight, queries, out_grad,
        spans, D // HEADS,
    )
    came = swap(partial_other)
    partial_own = return_own(place, key_grad, value_grad, key_weight, value_weight)
    shape = (ref_count, length, half)
    partial_own, came = partial_own.reshape(shape), came.reshape(shape)

    before = ()
    for phase in BACK:
        parts = spread(ref_of, place, partial_own, came, phase, nz)
        parts = [parts[0]] + [move(parts[j], 0, -j) for j in range(1, NY)]
        for step in phase:
            total = gather_grads(table, place, parts, phase, before, step, nz, rows_here)
            if step > 0:
                before = (move(total[0], 1, 0), move(total[1], -1, 0))
    return (query_grad, total[0])


def solution(mesh):
    return jax.shard_map(
        whole_step,
        mesh=mesh,
        in_specs=(
            P(("dp", "seq"), "head"),
            P(("dp", "seq"), "head"),
            P(("dp", "seq"), None, "head"),
            P(None, "head"),
            P(None, "head"),
            P(("dp", "seq"), None),
        ),
        out_specs=(P(("dp", "seq"), "head"), P(("dp", "seq"), None, "head")),
        check_vma=False,
    )
```

```python
import math

import jax
import jax.numpy as jnp
from jax import lax
from jax.experimental import pallas as pl
from jax.experimental.pallas import tpu as pltpu
from jax.sharding import PartitionSpec as P


D = 2048
HEADS = 16
NY = 4
CAP = 2
SPARE = 2
WIDE = 512


SMEM = pl.BlockSpec(memory_space=pltpu.SMEM)
VMEM = pl.BlockSpec(memory_space=pltpu.VMEM)
ANY = pl.BlockSpec(memory_space=pl.ANY)
BF = jnp.bfloat16
SMALL = pltpu.CompilerParams(vmem_limit_bytes=8 << 20)
F32 = jnp.float32

OUT = ((0, 1, 2), (3, 4))
BACK = ((4,), (3,), (2,), (1, 0))


def planes_of(step, nz):
    if step == 0 or 2 * step == nz:
        return (step,)
    return (step, nz - step)


def span_of(phase, nz):
    planes = sorted((d + nz // 2 - 1) % nz - (nz // 2 - 1) for t in phase for d in planes_of(t, nz))
    if nz // 2 - 1 in planes or nz // 2 in planes:
        planes = sorted(d % nz for d in planes)
    stride = planes[1] - planes[0] if len(planes) > 1 else 1
    assert planes == [planes[0] + stride * n for n in range(len(planes))]
    return planes[0], stride, len(planes)


def slots_of(phase, nz):
    first, stride, count = span_of(phase, nz)
    return [((first + stride * n) % nz, s) for n in range(count) for s in range(CAP)]


def ring(seq, dz, dy):
    nz = seq // NY
    pairs = []
    for z in range(nz):
        for y in range(NY):
            pairs.append((z * NY + y, ((z + dz) % nz) * NY + (y + dy) % NY))
    return pairs


def pick_rows(table, place, blocks, phase, nz):
    slots = slots_of(phase, nz)
    flat, where = [], {}
    for d, pieces in blocks.items():
        where[d] = []
        start = 0
        for a in pieces:
            where[d].append((len(flat), start, a.shape[0]))
            start += a.shape[0]
            flat.append(a)
    tail = flat[0].shape[1:]

    def body(t_ref, p_ref, *refs):
        ins, outs = refs[: len(flat)], refs[len(flat) :]
        for j in range(NY):
            for k, (d, s) in enumerate(slots):
                row = jnp.maximum(t_ref[j, (p_ref[0] + d) % nz * CAP + s], 0)
                if len(where[d]) == 1:
                    outs[j][k] = ins[where[d][0][0]][row]
                    continue
                for n, start, size in where[d]:

                    @pl.when((row >= start) & (row < start + size))
                    def _():
                        outs[j][k] = ins[n][jnp.clip(row - start, 0, size - 1)]

    return pl.pallas_call(
        body,
        in_specs=[SMEM, SMEM] + [VMEM] * len(flat),
        out_specs=[VMEM] * NY,
        out_shape=[jax.ShapeDtypeStruct((len(slots),) + tail, BF)] * NY,
        name="pick",
        compiler_params=SMALL,
    )(table, place, *flat)


def compact(ref_of, place, groups, nz, ref_count):
    flat = [a for group in groups for a in group]
    tail = flat[0].shape[1:]

    def body(r_ref, p_ref, *refs):
        ins, out = refs[:-1], refs[-1]
        for n, phase in enumerate(OUT):
            first, stride, count = span_of(phase, nz)

            def place_slots(k, carry):
                plane = (p_ref[0] + nz + first + stride * (k // CAP)) % nz
                at = [r_ref[j, plane * CAP + k % CAP] for j in range(NY)]
                for j in range(NY):
                    out[jnp.where(at[j] < 0, ref_count, at[j])] = ins[n * NY + j][k]
                return carry

            lax.fori_loop(0, count * CAP, place_slots, 0)

    return pl.pallas_call(
        body,
        in_specs=[SMEM, SMEM] + [VMEM] * len(flat),
        out_specs=VMEM,
        out_shape=jax.ShapeDtypeStruct((ref_count + SPARE,) + tail, BF),
        name="compact",
        compiler_params=SMALL,
    )(ref_of, place, *flat)


def spread(ref_of, place, own, other, phases, nz):
    tail = own.shape[1:]
    spans = [span_of(phase, nz) for phase in phases]

    def body(r_ref, p_ref, own_ref, other_ref, *outs):
        for n, (first, stride, count) in enumerate(spans):

            def place_slots(k, carry):
                plane = (p_ref[0] + nz + first + stride * (k // CAP)) % nz
                at = [jnp.maximum(r_ref[j, plane * CAP + k % CAP], 0) for j in range(NY)]
                for j in range(NY):
                    total = own_ref[at[j]] + other_ref[at[j]].astype(F32)
                    outs[n * NY + j][k] = total.astype(BF)
                return carry

            lax.fori_loop(0, count * CAP, place_slots, 0)

    flat = pl.pallas_call(
        body,
        in_specs=[SMEM, SMEM, VMEM, VMEM],
        out_specs=[VMEM] * (NY * len(phases)),
        out_shape=[
            jax.ShapeDtypeStruct((count * CAP,) + tail, BF) for *_, count in spans for _ in range(NY)
        ],
        compiler_params=SMALL,
        name="spread",
    )(ref_of, place, own, other)
    return [flat[n * NY : (n + 1) * NY] for n in range(len(phases))]


def gather_grads(table, place, parts, phase, before, step, nz, rows_here):
    planes = planes_of(step, nz)
    tail = parts[0].shape[1:]
    cut = rows_here // 2
    far = 2 * step == nz
    slots = slots_of(phase, nz)
    if far:
        shapes = [(cut,) + tail, (rows_here - cut,) + tail]
    else:
        shapes = [(rows_here,) + tail] * len(planes)
    halves = bool(before) and before[0].shape[0] != rows_here

    def body(t_ref, p_ref, *refs):
        ins = refs[:NY]
        prev = refs[NY : NY + len(before)]
        outs = refs[NY + len(before) : -1]
        acc = refs[-1]

        def fill(r, carry):
            for p in range(len(planes)):
                if step == 0:
                    acc[p, r] = prev[0][r].astype(F32) + prev[1][r].astype(F32)
                elif before and not halves:
                    acc[p, r] = prev[p][r].astype(F32)
                else:
                    acc[p, r] = jnp.zeros(tail, F32)
            return carry

        def low(r, carry):
            acc[0, r] = prev[0][r].astype(F32)
            return carry

        def high(r, carry):
            acc[1, r + cut] = prev[1][r].astype(F32)
            return carry

        lax.fori_loop(0, rows_here, fill, 0, unroll=2)
        if halves:
            lax.fori_loop(0, cut, low, 0)
            lax.fori_loop(0, rows_here - cut, high, 0)
        for p, d in enumerate(planes):
            at_plane = (p_ref[0] + d) % nz * CAP
            for j in range(NY):
                for s in range(CAP):
                    row = t_ref[j, at_plane + s]
                    k = slots.index((d, s))

                    @pl.when(row >= 0)
                    def _():
                        at = jnp.maximum(row, 0)
                        acc[p, at] = acc[p, at] + ins[j][k].astype(F32)

        def drain(r, carry):
            for p in range(len(planes)):
                outs[p][r] = acc[p, r].astype(BF)
            return carry

        def drain_low(r, carry):
            outs[0][r] = acc[0, r].astype(BF)
            return carry

        def drain_high(r, carry):
            outs[1][r] = acc[0, r + cut].astype(BF)
            return carry

        if far:
            lax.fori_loop(0, cut, drain_low, 0)
            lax.fori_loop(0, rows_here - cut, drain_high, 0)
        else:
            lax.fori_loop(0, rows_here, drain, 0, unroll=2)

    return pl.pallas_call(
        body,
        in_specs=[SMEM, SMEM] + [VMEM] * (NY + len(before)),
        out_specs=[VMEM] * len(shapes),
        out_shape=[jax.ShapeDtypeStruct(s, BF) for s in shapes],
        scratch_shapes=[pltpu.VMEM((len(planes), rows_here) + tail, F32)],
        compiler_params=SMALL,
        name="gather",
    )(table, place, *parts, *before)


def fetch(*arrays):
    count = len(arrays)

    def body(*refs):
        sem = refs[-1]
        copies = [
            pltpu.make_async_copy(refs[n], refs[count + n], sem.at[n]) for n in range(count)
        ]
        for copy in copies:
            copy.start()
        for copy in copies:
            copy.wait()

    return pl.pallas_call(
        body,
        in_specs=[pl.BlockSpec(memory_space=pltpu.HBM)] * count,
        out_specs=[VMEM] * count,
        out_shape=[pltpu.VMEM(a.shape, a.dtype) for a in arrays],
        scratch_shapes=[pltpu.SemaphoreType.DMA((count,))],
        compiler_params=SMALL,
        name="fetch",
    )(*arrays)


def project_own(place, own, key_weight, value_weight, rows):
    half = own.shape[1]

    def body(p_ref, own_ref, wk_ref, wv_ref, k_ref, v_ref):
        mine = pl.ds(pl.multiple_of(p_ref[2] * half, half), half)

        def block(n, carry):
            c = pl.ds(pl.multiple_of(n * WIDE, WIDE), WIDE)
            for w_ref, out in ((wk_ref, k_ref), (wv_ref, v_ref)):
                out[:, c] = jnp.dot(own_ref[:rows], w_ref[mine, c], preferred_element_type=F32)
            return carry

        lax.fori_loop(0, half // WIDE, block, 0)

    return pl.pallas_call(
        body,
        in_specs=[SMEM] + [VMEM] * 3,
        out_specs=[VMEM] * 2,
        out_shape=[jax.ShapeDtypeStruct((rows, half), F32)] * 2,
        compiler_params=SMALL,
        name="project_own",
    )(place, own, key_weight, value_weight)


def return_own(place, key_grad, value_grad, key_weight, value_weight):
    rows, half = key_grad.shape
    nt = (((1,), (1,)), ((), ()))

    def body(p_ref, dk_ref, dv_ref, wk_ref, wv_ref, out):
        def block(n, carry):
            c = pl.ds(pl.multiple_of(n * WIDE, WIDE), WIDE)
            at = pl.ds(pl.multiple_of(p_ref[2] * half + n * WIDE, WIDE), WIDE)
            total = lax.dot_general(dk_ref[...], wk_ref[at, :], nt, preferred_element_type=F32)
            total += lax.dot_general(dv_ref[...], wv_ref[at, :], nt, preferred_element_type=F32)
            out[:, c] = total
            return carry

        lax.fori_loop(0, half // WIDE, block, 0)

    return pl.pallas_call(
        body,
        in_specs=[SMEM] + [VMEM] * 4,
        out_specs=VMEM,
        out_shape=jax.ShapeDtypeStruct((rows, half), F32),
        compiler_params=SMALL,
        name="return_own",
    )(place, key_grad, value_grad, key_weight, value_weight)


def into_vmem(*arrays):
    held = fetch(*(pltpu.with_memory_space_constraint(a, pltpu.HBM) for a in arrays))
    return [pltpu.with_memory_space_constraint(a, pltpu.VMEM) for a in held]


def core_step(
    place, key_part, value_part, other, key_weight, value_weight, queries, out_grad, spans, head_size
):
    rows, half = key_part.shape
    tok = queries.shape[0] // spans
    per = rows // spans
    heads = half // head_size
    scaling = 1.0 / math.sqrt(head_size)
    nt = (((1,), (1,)), ((), ()))
    tn = (((0,), (0,)), ((), ()))
    cols = [slice(n * head_size, (n + 1) * head_size) for n in range(heads)]

    def body(
        p_ref, ka_ref, va_ref, oth_ref, wk_ref, wv_ref, q_ref, g_ref,
        dq_hbm, poth_ref, dk_ref, dv_ref, dq_ref, k_ref, v_ref, sem,
    ):
        theirs = pl.ds(pl.multiple_of((1 - p_ref[2]) * half, half), half)

        def project(n, carry):
            c = pl.ds(pl.multiple_of(n * half, half), half)
            for part, w_ref, out in ((ka_ref, wk_ref, k_ref), (va_ref, wv_ref, v_ref)):
                total = jnp.dot(oth_ref[:rows], w_ref[theirs, c], preferred_element_type=F32)
                out[:, c] = (part[:, c] + total).astype(BF)
            return carry

        lax.fori_loop(0, half // half, project, 0)

        def at(u):
            return (
                pl.ds(pl.multiple_of(u * per, per), per),
                pl.ds(pl.multiple_of(u * tok, tok), tok),
            )

        def weigh(u):
            here, there = at(u)
            probs_b, ds = [], []
            scores = [
                lax.dot_general(k_ref[here, c], q_ref[there, c], nt, preferred_element_type=F32)
                for c in cols
            ]
            dprobs = [
                lax.dot_general(v_ref[here, c], g_ref[there, c], nt, preferred_element_type=F32)
                for c in cols
            ]
            for sc, dp in zip(scores, dprobs):
                sc = sc * scaling
                raised = jnp.exp(sc - jnp.max(sc, axis=0, keepdims=True))
                probs = raised / jnp.sum(raised, axis=0, keepdims=True)
                pb = probs.astype(BF)
                delta = jnp.sum(pb.astype(F32) * dp, axis=0, keepdims=True)
                probs_b.append(pb)
                ds.append((probs * (dp - delta)).astype(BF))
            return tuple(probs_b), tuple(ds)

        def grads(u, probs_b, ds):
            here, there = at(u)
            for n, c in enumerate(cols):
                q, g, k = q_ref[there, c], g_ref[there, c], k_ref[here, c]
                dk = jnp.dot(ds[n], q, preferred_element_type=F32) * scaling
                dv = jnp.dot(probs_b[n], g, preferred_element_type=F32)
                dq = lax.dot_general(ds[n], k, tn, preferred_element_type=F32) * scaling
                dk_ref[here, c] = dk.astype(BF)
                dv_ref[here, c] = dv.astype(BF)
                dq_ref[there, c] = dq.astype(BF)

        def both(u, carry):
            after = weigh(u + 1)
            grads(u, *carry)
            return after

        grads(spans - 1, *lax.fori_loop(0, spans - 1, both, weigh(0)))
        store = pltpu.make_async_copy(dq_ref, dq_hbm, sem.at[0])
        store.start()

        def back(n, carry):
            c = pl.ds(pl.multiple_of(n * half, half), half)
            at_rows = pl.ds(pl.multiple_of((1 - p_ref[2]) * half + n * half, half), half)
            total = lax.dot_general(
                dk_ref[...], wk_ref[at_rows, :], nt, preferred_element_type=F32
            )
            total += lax.dot_general(
                dv_ref[...], wv_ref[at_rows, :], nt, preferred_element_type=F32
            )
            poth_ref[:, c] = total.astype(BF)
            return carry

        lax.fori_loop(0, half // half, back, 0)
        store.wait()

    return pl.pallas_call(
        body,
        in_specs=[SMEM] + [VMEM] * 7,
        out_specs=[ANY] + [VMEM] * 3,
        compiler_params=pltpu.CompilerParams(vmem_limit_bytes=16 << 20),
        out_shape=[
            jax.ShapeDtypeStruct(queries.shape, BF),
        ]
        + [jax.ShapeDtypeStruct((rows, half), BF)] * 3,
        scratch_shapes=[pltpu.VMEM(queries.shape, BF)]
        + [pltpu.VMEM((rows, half), BF)] * 2
        + [pltpu.SemaphoreType.DMA((1,))],
        name="core_step",
    )(place, key_part, value_part, other, key_weight, value_weight, queries, out_grad)


def slot_tables(ids, y0, nz, rows_here):
    count = ids.shape[1]
    owner = ids // rows_here
    local = ids % rows_here
    plane = owner // NY
    column = owner % NY
    refs = jnp.arange(count, dtype=jnp.int32)
    same = (owner[:, :, None] == owner[:, None, :]) & (refs[None, None, :] < refs[None, :, None])
    rank = jnp.sum(same.astype(jnp.int32), axis=2)
    code = plane * CAP + rank
    slots = jnp.arange(nz * CAP, dtype=jnp.int32)
    hit = (slots[None, :, None] == code[:, None, :]) & (column == y0)[:, None, :]
    table = jnp.sum(jnp.where(hit, local[:, None, :] + 1, 0), axis=2) - 1
    back = (y0 - column[0]) % NY
    sides = jnp.arange(NY, dtype=jnp.int32)
    mine = (slots[None, :, None] == code[0][None, None, :]) & (
        sides[:, None, None] == back[None, None, :]
    )
    ref_of = jnp.sum(jnp.where(mine, refs[None, None, :] + 1, 0), axis=2) - 1
    return table, ref_of


def whole_step(queries, out_grad, encodings, key_weight, value_weight, neighbours):
    seq = lax.axis_size("seq")
    nz = seq // NY
    far = nz // 2
    index = lax.axis_index("seq")
    head = lax.axis_index("head").astype(jnp.int32)
    z0 = index // NY
    y0 = index % NY
    spans = neighbours.shape[0]
    ref_count = 2 * spans
    rows_here, length, half = encodings.shape
    cut = rows_here // 2

    def move(x, dz, dy):
        return lax.ppermute(x, "seq", ring(seq, dz, dy))

    def swap(x):
        return lax.ppermute(x, "head", [(0, 1), (1, 0)])

    place = jnp.stack([z0, y0, head]).astype(jnp.int32)

    blocks = {0: into_vmem(encodings)}
    ahead = behind = encodings
    readers = None
    for step in range(1, far + 1):
        if step == far:
            ahead, behind = lax.optimization_barrier((ahead[cut:], behind[:cut]))
        behind = move(behind, 1, 0)
        ahead = move(ahead, -1, 0)
        if step == far:
            blocks[far] = [behind, ahead]
        else:
            blocks[step], blocks[nz - step] = [ahead], [behind]
        if readers is None:
            ids = neighbours.reshape(1, ref_count)
            two = jnp.concatenate([ids, move(ids, 0, -1)], axis=0)
            readers = jnp.concatenate([two, move(two, 0, -2)], axis=0)
            table, ref_of = slot_tables(readers, y0, nz, rows_here)
    groups = []
    for phase in OUT:
        need = {d: blocks[d] for step in phase for d in planes_of(step, nz)}
        picked = pick_rows(table, place, need, phase, nz)
        groups.append([picked[0]] + [move(picked[j], 0, j) for j in range(1, NY)])

    key_weight, value_weight, queries, out_grad = into_vmem(
        key_weight, value_weight, queries, out_grad
    )
    flat = (ref_count * length, half)
    own = compact(ref_of, place, groups, nz, ref_count)
    other = swap(own)
    parts = project_own(place, own.reshape(-1, half), key_weight, value_weight, flat[0])
    query_grad, partial_other, key_grad, value_grad = core_step(
        place, *parts, other.reshape(-1, half), key_weight, value_weight, queries, out_grad,
        spans, D // HEADS,
    )
    came = swap(partial_other)
    partial_own = return_own(place, key_grad, value_grad, key_weight, value_weight)
    shape = (ref_count, length, half)
    partial_own, came = partial_own.reshape(shape), came.reshape(shape)

    before = ()
    for n, phase in enumerate(BACK):
        if n in (0, len(BACK) - 1):
            ahead = BACK[n:] if n else BACK[:-1]
            sends = dict(enumerate(spread(ref_of, place, partial_own, came, ahead, nz), n))
        parts = sends[n]
        parts = [parts[0]] + [move(parts[j], 0, -j) for j in range(1, NY)]
        for step in phase:
            total = gather_grads(table, place, parts, phase, before, step, nz, rows_here)
            if step > 0:
                before = (move(total[0], 1, 0), move(total[1], -1, 0))
    return (query_grad, total[0])


def solution(mesh):
    return jax.shard_map(
        whole_step,
        mesh=mesh,
        in_specs=(
            P(("dp", "seq"), "head"),
            P(("dp", "seq"), "head"),
            P(("dp", "seq"), None, "head"),
            P(None, "head"),
            P(None, "head"),
            P(("dp", "seq"), None),
        ),
        out_specs=(P(("dp", "seq"), "head"), P(("dp", "seq"), None, "head")),
        check_vma=False,
    )
```

```python
import math

import jax
import jax.numpy as jnp
from jax import lax
from jax.experimental import pallas as pl
from jax.experimental.pallas import tpu as pltpu
from jax.sharding import PartitionSpec as P


D = 2048
HEADS = 16
NY = 4
CAP = 2
SPARE = 2


SPREADS = {0: 1, 1: 3, 3: 4}

SMEM = pl.BlockSpec(memory_space=pltpu.SMEM)
VMEM = pl.BlockSpec(memory_space=pltpu.VMEM)
ANY = pl.BlockSpec(memory_space=pl.ANY)
BF = jnp.bfloat16
SMALL = pltpu.CompilerParams(vmem_limit_bytes=8 << 20)
F32 = jnp.float32

OUT = ((0, 1, 2), (3, 4))
BACK = ((4,), (3,), (2,), (1, 0))


def planes_of(step, nz):
    if step == 0 or 2 * step == nz:
        return (step,)
    return (step, nz - step)


def span_of(phase, nz):
    planes = sorted((d + nz // 2 - 1) % nz - (nz // 2 - 1) for t in phase for d in planes_of(t, nz))
    if nz // 2 - 1 in planes or nz // 2 in planes:
        planes = sorted(d % nz for d in planes)
    stride = planes[1] - planes[0] if len(planes) > 1 else 1
    assert planes == [planes[0] + stride * n for n in range(len(planes))]
    return planes[0], stride, len(planes)


def slots_of(phase, nz):
    first, stride, count = span_of(phase, nz)
    return [((first + stride * n) % nz, s) for n in range(count) for s in range(CAP)]


def ring(seq, dz, dy):
    nz = seq // NY
    pairs = []
    for z in range(nz):
        for y in range(NY):
            pairs.append((z * NY + y, ((z + dz) % nz) * NY + (y + dy) % NY))
    return pairs


def pick_rows(table, place, blocks, phase, nz):
    slots = slots_of(phase, nz)
    flat, where = [], {}
    for d, pieces in blocks.items():
        where[d] = []
        start = 0
        for a in pieces:
            where[d].append((len(flat), start, a.shape[0]))
            start += a.shape[0]
            flat.append(a)
    tail = flat[0].shape[1:]

    def body(t_ref, p_ref, *refs):
        ins, outs = refs[: len(flat)], refs[len(flat) :]
        for j in range(NY):
            for k, (d, s) in enumerate(slots):
                row = jnp.maximum(t_ref[j, (p_ref[0] + d) % nz * CAP + s], 0)
                if len(where[d]) == 1:
                    outs[j][k] = ins[where[d][0][0]][row]
                    continue
                for n, start, size in where[d]:

                    @pl.when((row >= start) & (row < start + size))
                    def _():
                        outs[j][k] = ins[n][jnp.clip(row - start, 0, size - 1)]

    return pl.pallas_call(
        body,
        in_specs=[SMEM, SMEM] + [VMEM] * len(flat),
        out_specs=[VMEM] * NY,
        out_shape=[jax.ShapeDtypeStruct((len(slots),) + tail, BF)] * NY,
        name="pick",
        compiler_params=SMALL,
    )(table, place, *flat)


def compact(ref_of, place, groups, nz, ref_count):
    flat = [a for group in groups for a in group]
    tail = flat[0].shape[1:]

    def body(r_ref, p_ref, *refs):
        ins, out = refs[:-1], refs[-1]
        for n, phase in enumerate(OUT):
            first, stride, count = span_of(phase, nz)

            def place_slots(k, carry):
                plane = (p_ref[0] + nz + first + stride * (k // CAP)) % nz
                at = [r_ref[j, plane * CAP + k % CAP] for j in range(NY)]
                for j in range(NY):
                    out[jnp.where(at[j] < 0, ref_count, at[j])] = ins[n * NY + j][k]
                return carry

            lax.fori_loop(0, count * CAP, place_slots, 0)

    return pl.pallas_call(
        body,
        in_specs=[SMEM, SMEM] + [VMEM] * len(flat),
        out_specs=VMEM,
        out_shape=jax.ShapeDtypeStruct((ref_count + SPARE,) + tail, BF),
        name="compact",
        compiler_params=SMALL,
    )(ref_of, place, *flat)


def spread(ref_of, place, own, other, phases, nz):
    tail = own.shape[1:]
    spans = [span_of(phase, nz) for phase in phases]

    def body(r_ref, p_ref, own_ref, other_ref, *outs):
        for n, (first, stride, count) in enumerate(spans):

            def place_slots(k, carry):
                plane = (p_ref[0] + nz + first + stride * (k // CAP)) % nz
                at = [jnp.maximum(r_ref[j, plane * CAP + k % CAP], 0) for j in range(NY)]
                for j in range(NY):
                    total = own_ref[at[j]] + other_ref[at[j]].astype(F32)
                    outs[n * NY + j][k] = total.astype(BF)
                return carry

            lax.fori_loop(0, count * CAP, place_slots, 0)

    flat = pl.pallas_call(
        body,
        in_specs=[SMEM, SMEM, VMEM, VMEM],
        out_specs=[VMEM] * (NY * len(phases)),
        out_shape=[
            jax.ShapeDtypeStruct((count * CAP,) + tail, BF) for *_, count in spans for _ in range(NY)
        ],
        compiler_params=SMALL,
        name="spread",
    )(ref_of, place, own, other)
    return [flat[n * NY : (n + 1) * NY] for n in range(len(phases))]


def gather_grads(table, place, parts, phase, before, step, nz, rows_here):
    planes = planes_of(step, nz)
    tail = parts[0].shape[1:]
    cut = rows_here // 2
    far = 2 * step == nz
    slots = slots_of(phase, nz)
    if far:
        shapes = [(cut,) + tail, (rows_here - cut,) + tail]
    else:
        shapes = [(rows_here,) + tail] * len(planes)
    halves = bool(before) and before[0].shape[0] != rows_here

    def body(t_ref, p_ref, *refs):
        ins = refs[:NY]
        prev = refs[NY : NY + len(before)]
        outs = refs[NY + len(before) : -1]
        acc = refs[-1]

        def fill(r, carry):
            for p in range(len(planes)):
                if step == 0:
                    acc[p, r] = prev[0][r].astype(F32) + prev[1][r].astype(F32)
                elif before and not halves:
                    acc[p, r] = prev[p][r].astype(F32)
                else:
                    acc[p, r] = jnp.zeros(tail, F32)
            return carry

        def low(r, carry):
            acc[0, r] = prev[0][r].astype(F32)
            return carry

        def high(r, carry):
            acc[1, r + cut] = prev[1][r].astype(F32)
            return carry

        lax.fori_loop(0, rows_here, fill, 0, unroll=2)
        if halves:
            lax.fori_loop(0, cut, low, 0)
            lax.fori_loop(0, rows_here - cut, high, 0)
        for p, d in enumerate(planes):
            at_plane = (p_ref[0] + d) % nz * CAP
            for j in range(NY):
                for s in range(CAP):
                    row = t_ref[j, at_plane + s]
                    k = slots.index((d, s))

                    @pl.when(row >= 0)
                    def _():
                        at = jnp.maximum(row, 0)
                        acc[p, at] = acc[p, at] + ins[j][k].astype(F32)

        def drain(r, carry):
            for p in range(len(planes)):
                outs[p][r] = acc[p, r].astype(BF)
            return carry

        def drain_low(r, carry):
            outs[0][r] = acc[0, r].astype(BF)
            return carry

        def drain_high(r, carry):
            outs[1][r] = acc[0, r + cut].astype(BF)
            return carry

        if far:
            lax.fori_loop(0, cut, drain_low, 0)
            lax.fori_loop(0, rows_here - cut, drain_high, 0)
        else:
            lax.fori_loop(0, rows_here, drain, 0, unroll=2)

    return pl.pallas_call(
        body,
        in_specs=[SMEM, SMEM] + [VMEM] * (NY + len(before)),
        out_specs=[VMEM] * len(shapes),
        out_shape=[jax.ShapeDtypeStruct(s, BF) for s in shapes],
        scratch_shapes=[pltpu.VMEM((len(planes), rows_here) + tail, F32)],
        compiler_params=SMALL,
        name="gather",
    )(table, place, *parts, *before)


def fetch(*arrays):
    count = len(arrays)

    def body(*refs):
        sem = refs[-1]
        copies = [
            pltpu.make_async_copy(refs[n], refs[count + n], sem.at[n]) for n in range(count)
        ]
        for copy in copies:
            copy.start()
        for copy in copies:
            copy.wait()

    return pl.pallas_call(
        body,
        in_specs=[pl.BlockSpec(memory_space=pltpu.HBM)] * count,
        out_specs=[VMEM] * count,
        out_shape=[pltpu.VMEM(a.shape, a.dtype) for a in arrays],
        scratch_shapes=[pltpu.SemaphoreType.DMA((count,))],
        compiler_params=SMALL,
        name="fetch",
    )(*arrays)


def project_own(place, own, key_weight, value_weight, rows):
    half = own.shape[1]

    def body(p_ref, own_ref, wk_ref, wv_ref, k_ref, v_ref):
        mine = pl.ds(pl.multiple_of(p_ref[2] * half, half), half)

        def block(n, carry):
            c = pl.ds(pl.multiple_of(n * half, half), half)
            for w_ref, out in ((wk_ref, k_ref), (wv_ref, v_ref)):
                out[:, c] = jnp.dot(own_ref[:rows], w_ref[mine, c], preferred_element_type=F32)
            return carry

        lax.fori_loop(0, 1, block, 0)

    return pl.pallas_call(
        body,
        in_specs=[SMEM] + [VMEM] * 3,
        out_specs=[VMEM] * 2,
        out_shape=[jax.ShapeDtypeStruct((rows, half), F32)] * 2,
        compiler_params=SMALL,
        name="project_own",
    )(place, own, key_weight, value_weight)


def return_own(place, key_grad, value_grad, key_weight, value_weight):
    rows, half = key_grad.shape
    nt = (((1,), (1,)), ((), ()))

    def body(p_ref, dk_ref, dv_ref, wk_ref, wv_ref, out):
        def block(n, carry):
            c = pl.ds(pl.multiple_of(n * half, half), half)
            at = pl.ds(pl.multiple_of(p_ref[2] * half + n * half, half), half)
            total = lax.dot_general(dk_ref[...], wk_ref[at, :], nt, preferred_element_type=F32)
            total += lax.dot_general(dv_ref[...], wv_ref[at, :], nt, preferred_element_type=F32)
            out[:, c] = total
            return carry

        lax.fori_loop(0, 1, block, 0)

    return pl.pallas_call(
        body,
        in_specs=[SMEM] + [VMEM] * 4,
        out_specs=VMEM,
        out_shape=jax.ShapeDtypeStruct((rows, half), F32),
        compiler_params=SMALL,
        name="return_own",
    )(place, key_grad, value_grad, key_weight, value_weight)


def into_vmem(*arrays):
    held = fetch(*(pltpu.with_memory_space_constraint(a, pltpu.HBM) for a in arrays))
    return [pltpu.with_memory_space_constraint(a, pltpu.VMEM) for a in held]


def core_step(
    place, key_part, value_part, other, key_weight, value_weight, queries, out_grad, spans, head_size
):
    rows, half = key_part.shape
    tok = queries.shape[0] // spans
    per = rows // spans
    heads = half // head_size
    scaling = 1.0 / math.sqrt(head_size)
    nt = (((1,), (1,)), ((), ()))
    tn = (((0,), (0,)), ((), ()))
    cols = [slice(n * head_size, (n + 1) * head_size) for n in range(heads)]

    def body(
        p_ref, ka_ref, va_ref, oth_ref, wk_ref, wv_ref, q_ref, g_ref,
        dq_hbm, poth_ref, dk_ref, dv_ref, dq_ref, k_ref, v_ref, sem,
    ):
        theirs = pl.ds(pl.multiple_of((1 - p_ref[2]) * half, half), half)

        def project(n, carry):
            c = pl.ds(pl.multiple_of(n * half, half), half)
            for part, w_ref, out in ((ka_ref, wk_ref, k_ref), (va_ref, wv_ref, v_ref)):
                total = jnp.dot(oth_ref[:rows], w_ref[theirs, c], preferred_element_type=F32)
                out[:, c] = (part[:, c] + total).astype(BF)
            return carry

        lax.fori_loop(0, half // half, project, 0)

        def at(u):
            return (
                pl.ds(pl.multiple_of(u * per, per), per),
                pl.ds(pl.multiple_of(u * tok, tok), tok),
            )

        def weigh(u):
            here, there = at(u)
            probs_b, ds = [], []
            scores = [
                lax.dot_general(k_ref[here, c], q_ref[there, c], nt, preferred_element_type=F32)
                for c in cols
            ]
            dprobs = [
                lax.dot_general(v_ref[here, c], g_ref[there, c], nt, preferred_element_type=F32)
                for c in cols
            ]
            for sc, dp in zip(scores, dprobs):
                sc = sc * scaling
                raised = jnp.exp(sc - jnp.max(sc, axis=0, keepdims=True))
                probs = raised / jnp.sum(raised, axis=0, keepdims=True)
                pb = probs.astype(BF)
                delta = jnp.sum(pb.astype(F32) * dp, axis=0, keepdims=True)
                probs_b.append(pb)
                ds.append((probs * (dp - delta)).astype(BF))
            return tuple(probs_b), tuple(ds)

        def grads(u, probs_b, ds):
            here, there = at(u)
            for n, c in enumerate(cols):
                q, g, k = q_ref[there, c], g_ref[there, c], k_ref[here, c]
                dk = jnp.dot(ds[n], q, preferred_element_type=F32) * scaling
                dv = jnp.dot(probs_b[n], g, preferred_element_type=F32)
                dq = lax.dot_general(ds[n], k, tn, preferred_element_type=F32) * scaling
                dk_ref[here, c] = dk.astype(BF)
                dv_ref[here, c] = dv.astype(BF)
                dq_ref[there, c] = dq.astype(BF)

        def both(u, carry):
            after = weigh(u + 1)
            grads(u, *carry)
            return after

        grads(spans - 1, *lax.fori_loop(0, spans - 1, both, weigh(0)))
        store = pltpu.make_async_copy(dq_ref, dq_hbm, sem.at[0])
        store.start()

        def back(n, carry):
            c = pl.ds(pl.multiple_of(n * half, half), half)
            at_rows = pl.ds(pl.multiple_of((1 - p_ref[2]) * half + n * half, half), half)
            total = lax.dot_general(
                dk_ref[...], wk_ref[at_rows, :], nt, preferred_element_type=F32
            )
            total += lax.dot_general(
                dv_ref[...], wv_ref[at_rows, :], nt, preferred_element_type=F32
            )
            poth_ref[:, c] = total.astype(BF)
            return carry

        lax.fori_loop(0, half // half, back, 0)
        store.wait()

    return pl.pallas_call(
        body,
        in_specs=[SMEM] + [VMEM] * 7,
        out_specs=[ANY] + [VMEM] * 3,
        compiler_params=pltpu.CompilerParams(vmem_limit_bytes=16 << 20),
        out_shape=[
            jax.ShapeDtypeStruct(queries.shape, BF),
        ]
        + [jax.ShapeDtypeStruct((rows, half), BF)] * 3,
        scratch_shapes=[pltpu.VMEM(queries.shape, BF)]
        + [pltpu.VMEM((rows, half), BF)] * 2
        + [pltpu.SemaphoreType.DMA((1,))],
        name="core_step",
    )(place, key_part, value_part, other, key_weight, value_weight, queries, out_grad)


def slot_tables(ids, y0, nz, rows_here):
    count = ids.shape[1]
    owner = ids // rows_here
    local = ids % rows_here
    plane = owner // NY
    column = owner % NY
    refs = jnp.arange(count, dtype=jnp.int32)
    same = (owner[:, :, None] == owner[:, None, :]) & (refs[None, None, :] < refs[None, :, None])
    rank = jnp.sum(same.astype(jnp.int32), axis=2)
    code = plane * CAP + rank
    slots = jnp.arange(nz * CAP, dtype=jnp.int32)
    hit = (slots[None, :, None] == code[:, None, :]) & (column == y0)[:, None, :]
    table = jnp.sum(jnp.where(hit, local[:, None, :] + 1, 0), axis=2) - 1
    back = (y0 - column[0]) % NY
    sides = jnp.arange(NY, dtype=jnp.int32)
    mine = (slots[None, :, None] == code[0][None, None, :]) & (
        sides[:, None, None] == back[None, None, :]
    )
    ref_of = jnp.sum(jnp.where(mine, refs[None, None, :] + 1, 0), axis=2) - 1
    return table, ref_of


def whole_step(queries, out_grad, encodings, key_weight, value_weight, neighbours):
    seq = lax.axis_size("seq")
    nz = seq // NY
    far = nz // 2
    index = lax.axis_index("seq")
    head = lax.axis_index("head").astype(jnp.int32)
    z0 = index // NY
    y0 = index % NY
    spans = neighbours.shape[0]
    ref_count = 2 * spans
    rows_here, length, half = encodings.shape
    cut = rows_here // 2

    def move(x, dz, dy):
        return lax.ppermute(x, "seq", ring(seq, dz, dy))

    def swap(x):
        return lax.ppermute(x, "head", [(0, 1), (1, 0)])

    place = jnp.stack([z0, y0, head]).astype(jnp.int32)

    blocks = {0: into_vmem(encodings)}
    ahead = behind = encodings
    readers = None
    for step in range(1, far + 1):
        if step == far:
            ahead, behind = lax.optimization_barrier((ahead[cut:], behind[:cut]))
        behind = move(behind, 1, 0)
        ahead = move(ahead, -1, 0)
        if step == far:
            blocks[far] = [behind, ahead]
        else:
            blocks[step], blocks[nz - step] = [ahead], [behind]
        if readers is None:
            ids = neighbours.reshape(1, ref_count)
            two = jnp.concatenate([ids, move(ids, 0, -1)], axis=0)
            readers = jnp.concatenate([two, move(two, 0, -2)], axis=0)
            table, ref_of = slot_tables(readers, y0, nz, rows_here)
    groups = []
    for phase in OUT:
        need = {d: blocks[d] for step in phase for d in planes_of(step, nz)}
        picked = pick_rows(table, place, need, phase, nz)
        groups.append([picked[0]] + [move(picked[j], 0, j) for j in range(1, NY)])

    key_weight, value_weight, queries, out_grad = into_vmem(
        key_weight, value_weight, queries, out_grad
    )
    flat = (ref_count * length, half)
    own = compact(ref_of, place, groups, nz, ref_count)
    other = swap(own)
    parts = project_own(place, own.reshape(-1, half), key_weight, value_weight, flat[0])
    query_grad, partial_other, key_grad, value_grad = core_step(
        place, *parts, other.reshape(-1, half), key_weight, value_weight, queries, out_grad,
        spans, D // HEADS,
    )
    came = swap(partial_other)
    partial_own = return_own(place, key_grad, value_grad, key_weight, value_weight)
    shape = (ref_count, length, half)
    partial_own, came = partial_own.reshape(shape), came.reshape(shape)

    before = ()
    for n, phase in enumerate(BACK):
        if n in SPREADS:
            some = BACK[n : SPREADS[n]]
            sends = dict(enumerate(spread(ref_of, place, partial_own, came, some, nz), n))
        parts = sends[n]
        parts = [parts[0]] + [move(parts[j], 0, -j) for j in range(1, NY)]
        for step in phase:
            total = gather_grads(table, place, parts, phase, before, step, nz, rows_here)
            if step > 0:
                before = (move(total[0], 1, 0), move(total[1], -1, 0))
    return (query_grad, total[0])


def solution(mesh):
    return jax.shard_map(
        whole_step,
        mesh=mesh,
        in_specs=(
            P(("dp", "seq"), "head"),
            P(("dp", "seq"), "head"),
            P(("dp", "seq"), None, "head"),
            P(None, "head"),
            P(None, "head"),
            P(("dp", "seq"), None),
        ),
        out_specs=(P(("dp", "seq"), "head"), P(("dp", "seq"), None, "head")),
        check_vma=False,
    )
```

```python
import math

import jax
import jax.numpy as jnp
from jax import lax
from jax.experimental import pallas as pl
from jax.experimental.pallas import tpu as pltpu
from jax.sharding import PartitionSpec as P


D = 2048
HEADS = 16
NY = 4
CAP = 2
SPARE = 2


SPREADS = {0: 1, 1: 3, 3: 4}

SMEM = pl.BlockSpec(memory_space=pltpu.SMEM)
VMEM = pl.BlockSpec(memory_space=pltpu.VMEM)
ANY = pl.BlockSpec(memory_space=pl.ANY)
BF = jnp.bfloat16
SMALL = pltpu.CompilerParams(vmem_limit_bytes=8 << 20)
F32 = jnp.float32

OUT = ((0, 1, 2), (3, 4))
BACK = ((4,), (3,), (2,), (1, 0))


def planes_of(step, nz):
    if step == 0 or 2 * step == nz:
        return (step,)
    return (step, nz - step)


def span_of(phase, nz):
    planes = sorted((d + nz // 2 - 1) % nz - (nz // 2 - 1) for t in phase for d in planes_of(t, nz))
    if nz // 2 - 1 in planes or nz // 2 in planes:
        planes = sorted(d % nz for d in planes)
    stride = planes[1] - planes[0] if len(planes) > 1 else 1
    assert planes == [planes[0] + stride * n for n in range(len(planes))]
    return planes[0], stride, len(planes)


def slots_of(phase, nz):
    first, stride, count = span_of(phase, nz)
    return [((first + stride * n) % nz, s) for n in range(count) for s in range(CAP)]


def ring(seq, dz, dy):
    nz = seq // NY
    pairs = []
    for z in range(nz):
        for y in range(NY):
            pairs.append((z * NY + y, ((z + dz) % nz) * NY + (y + dy) % NY))
    return pairs


def pick_rows(table, place, blocks, phase, nz):
    slots = slots_of(phase, nz)
    flat, where = [], {}
    for d, pieces in blocks.items():
        where[d] = []
        start = 0
        for a in pieces:
            where[d].append((len(flat), start, a.shape[0]))
            start += a.shape[0]
            flat.append(a)
    tail = flat[0].shape[1:]

    def body(t_ref, p_ref, *refs):
        ins, outs = refs[: len(flat)], refs[len(flat) :]
        for j in range(NY):
            for k, (d, s) in enumerate(slots):
                row = jnp.maximum(t_ref[j, (p_ref[0] + d) % nz * CAP + s], 0)
                if len(where[d]) == 1:
                    outs[j][k] = ins[where[d][0][0]][row]
                    continue
                for n, start, size in where[d]:

                    @pl.when((row >= start) & (row < start + size))
                    def _():
                        outs[j][k] = ins[n][jnp.clip(row - start, 0, size - 1)]

    return pl.pallas_call(
        body,
        in_specs=[SMEM, SMEM] + [VMEM] * len(flat),
        out_specs=[VMEM] * NY,
        out_shape=[jax.ShapeDtypeStruct((len(slots),) + tail, BF)] * NY,
        name="pick",
        compiler_params=SMALL,
    )(table, place, *flat)


def compact(ref_of, place, groups, nz, ref_count):
    flat = [a for group in groups for a in group]
    tail = flat[0].shape[1:]

    def body(r_ref, p_ref, *refs):
        ins, out = refs[:-1], refs[-1]
        for n, phase in enumerate(OUT):
            first, stride, count = span_of(phase, nz)

            def place_slots(k, carry):
                plane = (p_ref[0] + nz + first + stride * (k // CAP)) % nz
                at = [r_ref[j, plane * CAP + k % CAP] for j in range(NY)]
                for j in range(NY):
                    out[jnp.where(at[j] < 0, ref_count, at[j])] = ins[n * NY + j][k]
                return carry

            lax.fori_loop(0, count * CAP, place_slots, 0, unroll=2)

    return pl.pallas_call(
        body,
        in_specs=[SMEM, SMEM] + [VMEM] * len(flat),
        out_specs=VMEM,
        out_shape=jax.ShapeDtypeStruct((ref_count + SPARE,) + tail, BF),
        name="compact",
        compiler_params=SMALL,
    )(ref_of, place, *flat)


def spread(ref_of, place, own, other, phases, nz):
    tail = own.shape[1:]
    spans = [span_of(phase, nz) for phase in phases]

    def body(r_ref, p_ref, own_ref, other_ref, *outs):
        for n, (first, stride, count) in enumerate(spans):

            def place_slots(k, carry):
                plane = (p_ref[0] + nz + first + stride * (k // CAP)) % nz
                at = [jnp.maximum(r_ref[j, plane * CAP + k % CAP], 0) for j in range(NY)]
                for j in range(NY):
                    total = own_ref[at[j]] + other_ref[at[j]].astype(F32)
                    outs[n * NY + j][k] = total.astype(BF)
                return carry

            lax.fori_loop(0, count * CAP, place_slots, 0, unroll=2)

    flat = pl.pallas_call(
        body,
        in_specs=[SMEM, SMEM, VMEM, VMEM],
        out_specs=[VMEM] * (NY * len(phases)),
        out_shape=[
            jax.ShapeDtypeStruct((count * CAP,) + tail, BF) for *_, count in spans for _ in range(NY)
        ],
        compiler_params=SMALL,
        name="spread",
    )(ref_of, place, own, other)
    return [flat[n * NY : (n + 1) * NY] for n in range(len(phases))]


def gather_grads(table, place, parts, phase, before, step, nz, rows_here):
    planes = planes_of(step, nz)
    tail = parts[0].shape[1:]
    cut = rows_here // 2
    far = 2 * step == nz
    slots = slots_of(phase, nz)
    if far:
        shapes = [(cut,) + tail, (rows_here - cut,) + tail]
    else:
        shapes = [(rows_here,) + tail] * len(planes)
    halves = bool(before) and before[0].shape[0] != rows_here

    def body(t_ref, p_ref, *refs):
        ins = refs[:NY]
        prev = refs[NY : NY + len(before)]
        outs = refs[NY + len(before) : NY + len(before) + len(shapes)]
        acc = refs[NY + len(before) + len(shapes)]

        def fill(r, carry):
            for p in range(len(planes)):
                if step == 0:
                    acc[p, r] = prev[0][r].astype(F32) + prev[1][r].astype(F32)
                elif before and not halves:
                    acc[p, r] = prev[p][r].astype(F32)
                else:
                    acc[p, r] = jnp.zeros(tail, F32)
            return carry

        def low(r, carry):
            acc[0, r] = prev[0][r].astype(F32)
            return carry

        def high(r, carry):
            acc[1, r + cut] = prev[1][r].astype(F32)
            return carry

        lax.fori_loop(0, rows_here, fill, 0, unroll=2)
        if halves:
            lax.fori_loop(0, cut, low, 0)
            lax.fori_loop(0, rows_here - cut, high, 0)
        for p, d in enumerate(planes):
            at_plane = (p_ref[0] + d) % nz * CAP
            for j in range(NY):
                for s in range(CAP):
                    row = t_ref[j, at_plane + s]
                    k = slots.index((d, s))

                    @pl.when(row >= 0)
                    def _():
                        at = jnp.maximum(row, 0)
                        acc[p, at] = acc[p, at] + ins[j][k].astype(F32)

        def drain(r, carry):
            for p in range(len(planes)):
                outs[p][r] = acc[p, r].astype(BF)
            return carry

        def drain_low(r, carry):
            outs[0][r] = acc[0, r].astype(BF)
            return carry

        def drain_high(r, carry):
            outs[1][r] = acc[0, r + cut].astype(BF)
            return carry

        if far:
            lax.fori_loop(0, cut, drain_low, 0)
            lax.fori_loop(0, rows_here - cut, drain_high, 0)
        elif step == 0:
            done, sem = refs[-2:]
            stores = []
            for n, (start, stop) in enumerate(((0, cut), (cut, rows_here))):

                def finish(r, carry):
                    done[r] = acc[0, r].astype(BF)
                    return carry

                lax.fori_loop(start, stop, finish, 0)
                rows = slice(start, stop)
                stores.append(
                    pltpu.make_async_copy(done.at[rows], outs[0].at[rows], sem.at[n])
                )
                stores[-1].start()
            for store in stores:
                store.wait()
        else:
            lax.fori_loop(0, rows_here, drain, 0, unroll=2)

    return pl.pallas_call(
        body,
        in_specs=[SMEM, SMEM] + [VMEM] * (NY + len(before)),
        out_specs=[ANY if step == 0 else VMEM] * len(shapes),
        out_shape=[jax.ShapeDtypeStruct(s, BF) for s in shapes],
        scratch_shapes=[pltpu.VMEM((len(planes), rows_here) + tail, F32)]
        + ([pltpu.VMEM(shapes[0], BF), pltpu.SemaphoreType.DMA((2,))] if step == 0 else []),
        compiler_params=SMALL,
        name="gather",
    )(table, place, *parts, *before)


def fetch(*arrays):
    count = len(arrays)

    def body(*refs):
        sem = refs[-1]
        copies = [
            pltpu.make_async_copy(refs[n], refs[count + n], sem.at[n]) for n in range(count)
        ]
        for copy in copies:
            copy.start()
        for copy in copies:
            copy.wait()

    return pl.pallas_call(
        body,
        in_specs=[pl.BlockSpec(memory_space=pltpu.HBM)] * count,
        out_specs=[VMEM] * count,
        out_shape=[pltpu.VMEM(a.shape, a.dtype) for a in arrays],
        scratch_shapes=[pltpu.SemaphoreType.DMA((count,))],
        compiler_params=SMALL,
        name="fetch",
    )(*arrays)


def project_own(place, own, key_weight, value_weight, rows):
    half = own.shape[1]

    def body(p_ref, own_ref, wk_ref, wv_ref, k_ref, v_ref):
        mine = pl.ds(pl.multiple_of(p_ref[2] * half, half), half)

        def block(n, carry):
            c = pl.ds(pl.multiple_of(n * half, half), half)
            for w_ref, out in ((wk_ref, k_ref), (wv_ref, v_ref)):
                out[:, c] = jnp.dot(own_ref[:rows], w_ref[mine, c], preferred_element_type=F32)
            return carry

        lax.fori_loop(0, 1, block, 0)

    return pl.pallas_call(
        body,
        in_specs=[SMEM] + [VMEM] * 3,
        out_specs=[VMEM] * 2,
        out_shape=[jax.ShapeDtypeStruct((rows, half), F32)] * 2,
        compiler_params=SMALL,
        name="project_own",
    )(place, own, key_weight, value_weight)


def return_own(place, key_grad, value_grad, key_weight, value_weight):
    rows, half = key_grad.shape
    nt = (((1,), (1,)), ((), ()))

    def body(p_ref, dk_ref, dv_ref, wk_ref, wv_ref, out):
        def block(n, carry):
            c = pl.ds(pl.multiple_of(n * half, half), half)
            at = pl.ds(pl.multiple_of(p_ref[2] * half + n * half, half), half)
            total = lax.dot_general(dk_ref[...], wk_ref[at, :], nt, preferred_element_type=F32)
            total += lax.dot_general(dv_ref[...], wv_ref[at, :], nt, preferred_element_type=F32)
            out[:, c] = total
            return carry

        lax.fori_loop(0, 1, block, 0)

    return pl.pallas_call(
        body,
        in_specs=[SMEM] + [VMEM] * 4,
        out_specs=VMEM,
        out_shape=jax.ShapeDtypeStruct((rows, half), F32),
        compiler_params=SMALL,
        name="return_own",
    )(place, key_grad, value_grad, key_weight, value_weight)


def into_vmem(*arrays):
    held = fetch(*(pltpu.with_memory_space_constraint(a, pltpu.HBM) for a in arrays))
    return [pltpu.with_memory_space_constraint(a, pltpu.VMEM) for a in held]


def core_step(
    place, key_part, value_part, other, key_weight, value_weight, queries, out_grad, spans, head_size
):
    rows, half = key_part.shape
    tok = queries.shape[0] // spans
    per = rows // spans
    heads = half // head_size
    scaling = 1.0 / math.sqrt(head_size)
    nt = (((1,), (1,)), ((), ()))
    tn = (((0,), (0,)), ((), ()))
    cols = [slice(n * head_size, (n + 1) * head_size) for n in range(heads)]

    def body(
        p_ref, ka_ref, va_ref, oth_ref, wk_ref, wv_ref, q_ref, g_ref,
        dq_hbm, poth_ref, dk_ref, dv_ref, dq_ref, k_ref, v_ref, sem,
    ):
        theirs = pl.ds(pl.multiple_of((1 - p_ref[2]) * half, half), half)

        def project(n, carry):
            c = pl.ds(pl.multiple_of(n * half, half), half)
            for part, w_ref, out in ((ka_ref, wk_ref, k_ref), (va_ref, wv_ref, v_ref)):
                total = jnp.dot(oth_ref[:rows], w_ref[theirs, c], preferred_element_type=F32)
                out[:, c] = (part[:, c] + total).astype(BF)
            return carry

        lax.fori_loop(0, half // half, project, 0)

        def at(u):
            return (
                pl.ds(pl.multiple_of(u * per, per), per),
                pl.ds(pl.multiple_of(u * tok, tok), tok),
            )

        def weigh(u):
            here, there = at(u)
            probs_b, ds = [], []
            scores = [
                lax.dot_general(k_ref[here, c], q_ref[there, c], nt, preferred_element_type=F32)
                for c in cols
            ]
            dprobs = [
                lax.dot_general(v_ref[here, c], g_ref[there, c], nt, preferred_element_type=F32)
                for c in cols
            ]
            for sc, dp in zip(scores, dprobs):
                sc = sc * scaling
                raised = jnp.exp(sc - jnp.max(sc, axis=0, keepdims=True))
                probs = raised / jnp.sum(raised, axis=0, keepdims=True)
                pb = probs.astype(BF)
                delta = jnp.sum(pb.astype(F32) * dp, axis=0, keepdims=True)
                probs_b.append(pb)
                ds.append((probs * (dp - delta)).astype(BF))
            return tuple(probs_b), tuple(ds)

        def grads(u, probs_b, ds):
            here, there = at(u)
            for n, c in enumerate(cols):
                q, g, k = q_ref[there, c], g_ref[there, c], k_ref[here, c]
                dk = jnp.dot(ds[n], q, preferred_element_type=F32) * scaling
                dv = jnp.dot(probs_b[n], g, preferred_element_type=F32)
                dq = lax.dot_general(ds[n], k, tn, preferred_element_type=F32) * scaling
                dk_ref[here, c] = dk.astype(BF)
                dv_ref[here, c] = dv.astype(BF)
                dq_ref[there, c] = dq.astype(BF)

        def both(u, carry):
            after = weigh(u + 1)
            grads(u, *carry)
            return after

        grads(spans - 1, *lax.fori_loop(0, spans - 1, both, weigh(0), unroll=2))
        store = pltpu.make_async_copy(dq_ref, dq_hbm, sem.at[0])
        store.start()

        def back(n, carry):
            c = pl.ds(pl.multiple_of(n * half, half), half)
            at_rows = pl.ds(pl.multiple_of((1 - p_ref[2]) * half + n * half, half), half)
            total = lax.dot_general(
                dk_ref[...], wk_ref[at_rows, :], nt, preferred_element_type=F32
            )
            total += lax.dot_general(
                dv_ref[...], wv_ref[at_rows, :], nt, preferred_element_type=F32
            )
            poth_ref[:, c] = total.astype(BF)
            return carry

        lax.fori_loop(0, half // half, back, 0)
        store.wait()

    return pl.pallas_call(
        body,
        in_specs=[SMEM] + [VMEM] * 7,
        out_specs=[ANY] + [VMEM] * 3,
        compiler_params=pltpu.CompilerParams(vmem_limit_bytes=16 << 20),
        out_shape=[
            jax.ShapeDtypeStruct(queries.shape, BF),
        ]
        + [jax.ShapeDtypeStruct((rows, half), BF)] * 3,
        scratch_shapes=[pltpu.VMEM(queries.shape, BF)]
        + [pltpu.VMEM((rows, half), BF)] * 2
        + [pltpu.SemaphoreType.DMA((1,))],
        name="core_step",
    )(place, key_part, value_part, other, key_weight, value_weight, queries, out_grad)


def slot_tables(ids, y0, nz, rows_here):
    count = ids.shape[1]
    owner = ids // rows_here
    local = ids % rows_here
    plane = owner // NY
    column = owner % NY
    refs = jnp.arange(count, dtype=jnp.int32)
    same = (owner[:, :, None] == owner[:, None, :]) & (refs[None, None, :] < refs[None, :, None])
    rank = jnp.sum(same.astype(jnp.int32), axis=2)
    code = plane * CAP + rank
    slots = jnp.arange(nz * CAP, dtype=jnp.int32)
    hit = (slots[None, :, None] == code[:, None, :]) & (column == y0)[:, None, :]
    table = jnp.sum(jnp.where(hit, local[:, None, :] + 1, 0), axis=2) - 1
    back = (y0 - column[0]) % NY
    sides = jnp.arange(NY, dtype=jnp.int32)
    mine = (slots[None, :, None] == code[0][None, None, :]) & (
        sides[:, None, None] == back[None, None, :]
    )
    ref_of = jnp.sum(jnp.where(mine, refs[None, None, :] + 1, 0), axis=2) - 1
    return table, ref_of


def whole_step(queries, out_grad, encodings, key_weight, value_weight, neighbours):
    seq = lax.axis_size("seq")
    nz = seq // NY
    far = nz // 2
    index = lax.axis_index("seq")
    head = lax.axis_index("head").astype(jnp.int32)
    z0 = index // NY
    y0 = index % NY
    spans = neighbours.shape[0]
    ref_count = 2 * spans
    rows_here, length, half = encodings.shape
    cut = rows_here // 2

    def move(x, dz, dy):
        return lax.ppermute(x, "seq", ring(seq, dz, dy))

    def swap(x):
        return lax.ppermute(x, "head", [(0, 1), (1, 0)])

    place = jnp.stack([z0, y0, head]).astype(jnp.int32)

    blocks = {0: into_vmem(encodings)}
    ahead = behind = encodings
    readers = None
    for step in range(1, far + 1):
        if step == far:
            ahead, behind = lax.optimization_barrier((ahead[cut:], behind[:cut]))
        behind = move(behind, 1, 0)
        ahead = move(ahead, -1, 0)
        if step == far:
            blocks[far] = [behind, ahead]
        else:
            blocks[step], blocks[nz - step] = [ahead], [behind]
        if readers is None:
            ids = neighbours.reshape(1, ref_count)
            two = jnp.concatenate([ids, move(ids, 0, -1)], axis=0)
            readers = jnp.concatenate([two, move(two, 0, -2)], axis=0)
            table, ref_of = slot_tables(readers, y0, nz, rows_here)
    groups = []
    for phase in OUT:
        need = {d: blocks[d] for step in phase for d in planes_of(step, nz)}
        picked = pick_rows(table, place, need, phase, nz)
        groups.append([picked[0]] + [move(picked[j], 0, j) for j in range(1, NY)])

    key_weight, value_weight, queries, out_grad = into_vmem(
        key_weight, value_weight, queries, out_grad
    )
    flat = (ref_count * length, half)
    own = compact(ref_of, place, groups, nz, ref_count)
    other = swap(own)
    parts = project_own(place, own.reshape(-1, half), key_weight, value_weight, flat[0])
    query_grad, partial_other, key_grad, value_grad = core_step(
        place, *parts, other.reshape(-1, half), key_weight, value_weight, queries, out_grad,
        spans, D // HEADS,
    )
    came = swap(partial_other)
    partial_own = return_own(place, key_grad, value_grad, key_weight, value_weight)
    shape = (ref_count, length, half)
    partial_own, came = partial_own.reshape(shape), came.reshape(shape)

    before = ()
    for n, phase in enumerate(BACK):
        if n in SPREADS:
            some = BACK[n : SPREADS[n]]
            sends = dict(enumerate(spread(ref_of, place, partial_own, came, some, nz), n))
        parts = sends[n]
        parts = [parts[0]] + [move(parts[j], 0, -j) for j in range(1, NY)]
        for step in phase:
            total = gather_grads(table, place, parts, phase, before, step, nz, rows_here)
            if step > 0:
                before = (move(total[0], 1, 0), move(total[1], -1, 0))
    return (query_grad, total[0])


def solution(mesh):
    return jax.shard_map(
        whole_step,
        mesh=mesh,
        in_specs=(
            P(("dp", "seq"), "head"),
            P(("dp", "seq"), "head"),
            P(("dp", "seq"), None, "head"),
            P(None, "head"),
            P(None, "head"),
            P(("dp", "seq"), None),
        ),
        out_specs=(P(("dp", "seq"), "head"), P(("dp", "seq"), None, "head")),
        check_vma=False,
    )
```
